32 devices in a mesh: mesh: 8 (over z, x), sub: 4 (over y, core).
Axes of the slice: x: 2, y: 2, z: 4, core: 2. Of those that a mesh axis runs over, the one named last changes fastest.
Arguments:
- coords: float32 [3, 65536], P(None, ('mesh', 'sub')), may hold values from -6 to 6
- veloc: float32 [3, 65536], P(None, ('mesh', 'sub')), may hold values from -6 to 6
- node_mass: float32 [65536], P(('mesh', 'sub')), may hold values from 0.5 to 2
- stress: float32 [3, 131072], P(None, ('mesh', 'sub')), may hold values from -4 to 4
- connect: int32 [4, 131072], P(None, ('mesh', 'sub')), may hold values from 0 to 3071
- send_mesh: int32 [16384], P(('mesh', 'sub')), may hold values from 0 to 2047
- send_sub: int32 [16384], P(('mesh', 'sub')), may hold values from 0 to 2047
- send_pick: int32 [4, 512], P(None, ('mesh', 'sub')), may hold values from 0 to 31
- bucket_list: int32 [4, 4, 512], P(None, None, ('mesh', 'sub')), may hold values from 0 to 15
- pair_mask: int32 [4, 4, 65536], P(None, None, ('mesh', 'sub')), may hold values 0 or 1
Outputs:
- veloc_out: float32 [3, 65536], P(None, ('mesh', 'sub'))
- stress_out: float32 [3, 131072], P(None, ('mesh', 'sub'))
The draws below stay inside these ranges and needn't reach their ends.
Inputs may be any that keep to these rules, and one draw needn't show every extreme that they name: `connect`: columns below 2048 are own nodes, then 512 mesh ghosts, then 512 sub ghosts. `send_pick`: a block may be sent to several receivers and several places.
All inputs are finite; a program needn't handle non-finite values. No bound on the sum of `pair_mask` on one device may be relied on, other than what follows from the above.
Results may differ from the reference program's by a relative error of at most 0.0003.
Values sent between devices are 32-bit elements; how exact they have to be, the bound alone decides.
No kernel may reach another device: no remote copies, remote signals or barrier semaphores. Data moves between devices by JAX's collectives and lax.ppermute only.
A program may use at most 64 MiB of HBM per device.

```python
import math
import jax
import jax.numpy as jnp
from jax import lax

NODE_DEV = 2048
ELEM_DEV = 4096
GHOST_M = 512
GHOST_S = 512
SEG = 128
CAP = 2
CAND = 4
STEPS = 4
NODES = 65536
ELEMS = 131072
SLOTS = 16
PICKS = 512
BUCKETS = 512
N_MESH = 8
N_SUB = 4


def with_ends(values, key, low, largest):
    index_at = [jax.random.randint(jax.random.fold_in(key, axis), (), 0, length) for axis, length in enumerate(values.shape)]
    main_axis = values.shape.index(max(values.shape))
    beside = index_at[:main_axis] + [(index_at[main_axis] + 1) % values.shape[main_axis]] + index_at[main_axis + 1:]
    return values.at[tuple(index_at)].set(low).at[tuple(beside)].set(largest)


def levels(own_key, extent, shards, least, high):
    factor_of, own = 1.0, jax.random.fold_in(own_key, 6)
    for dim, parts in shards:
        draws = jnp.exp(jax.random.uniform(jax.random.fold_in(own, dim), (parts,), jnp.float32, least / len(shards), high / len(shards)))
        factor_of = factor_of * jnp.repeat(draws, extent[dim] // parts).reshape([-1 if axis == dim else 1 for axis in range(len(extent))])
    return factor_of


def centred(stream_key, dims, width, limit, cuts=(), held_as=jnp.bfloat16):
    drawn = width * jax.random.normal(stream_key, dims, jnp.float32)
    if cuts:
        drawn = drawn * levels(stream_key, dims, cuts, -0.22, 0.18)
    return jnp.clip(drawn, -limit, limit).astype(held_as)


def setup_inputs(seed: int = 0) -> dict:
    keys = jax.random.split(jax.random.key(seed), 11)
    coords = centred(keys[0], (3, NODES), 1.0, 6.0, ((1, 32),), jnp.float32)
    veloc = centred(keys[1], (3, NODES), 1.0, 6.0, ((1, 32),), jnp.float32)
    node_mass = jnp.clip(jnp.exp(math.log(2.0) - 1.3862944 * jax.random.uniform(keys[2], (NODES,), jnp.float32) ** levels(keys[2], (NODES,), ((0, 32),), -0.2, 0.2)), 0.5, 2.0)
    stress = centred(keys[3], (3, ELEMS), 0.5, 4.0, ((1, 32),), jnp.float32)
    connect = with_ends(jax.random.randint(keys[4], (4, ELEMS), 0, NODE_DEV + GHOST_M + GHOST_S), jax.random.fold_in(keys[4], 1), 0, (NODE_DEV + GHOST_M + GHOST_S) - 1).astype(jnp.int32)
    send_mesh = with_ends(jax.random.randint(keys[5], (GHOST_M * N_MESH * N_SUB,), 0, NODE_DEV), jax.random.fold_in(keys[5], 1), 0, NODE_DEV - 1).astype(jnp.int32)
    send_sub = with_ends(jax.random.randint(keys[6], (GHOST_S * N_MESH * N_SUB,), 0, NODE_DEV), jax.random.fold_in(keys[6], 1), 0, NODE_DEV - 1).astype(jnp.int32)
    send_pick = with_ends(jax.random.randint(keys[7], (STEPS, PICKS), 0, ELEM_DEV // SEG), jax.random.fold_in(keys[7], 1), 0, (ELEM_DEV // SEG) - 1).astype(jnp.int32)
    bucket_list = with_ends(jax.random.randint(keys[8], (STEPS, CAND, BUCKETS), 0, SLOTS), jax.random.fold_in(keys[8], 1), 0, SLOTS - 1).astype(jnp.int32)
    pair_mask = with_ends((jax.random.randint(keys[9], (STEPS, CAND, NODES), 0, 2) < 1).astype(jnp.int32), jax.random.fold_in(keys[9], 1), 0, 1)
    return {"coords": coords, "veloc": veloc, "node_mass": node_mass, "stress": stress, "connect": connect, "send_mesh": send_mesh, "send_sub": send_sub, "send_pick": send_pick, "bucket_list": bucket_list, "pair_mask": pair_mask}


TIME_STEP = 0.2
YOUNG = 1.0
POISSON = 0.3
HOURGLASS = 0.01
PENALTY = 0.2
REACH = 4.0
HIGH = lax.Precision.HIGHEST
HOUR_SIGNS = (1.0, -1.0, 1.0, -1.0)

def cross_rows(left_vec, right_vec):
    return jnp.stack([left_vec[1] * right_vec[2] - left_vec[2] * right_vec[1], left_vec[2] * right_vec[0] - left_vec[0] * right_vec[2], left_vec[0] * right_vec[1] - left_vec[1] * right_vec[0]])

def geometry(corner):
    diag_one = corner[:, 2] - corner[:, 0]
    diag_two = corner[:, 3] - corner[:, 1]
    normal_raw = cross_rows(diag_one, diag_two)
    twice_area = jnp.maximum(jnp.sqrt(lax.optimization_barrier(jnp.sum(normal_raw * normal_raw, axis=0))), 1.0)
    normal = normal_raw / twice_area
    centre = 0.25 * (corner[:, 0] + corner[:, 1] + corner[:, 2] + corner[:, 3])
    return (centre, normal, twice_area)

def shell_forces(corner, corner_vel, stress_now):
    centre, normal, twice_area = geometry(corner)
    side_raw = corner[:, 1] - corner[:, 0]
    side_len = jnp.maximum(jnp.sqrt(lax.optimization_barrier(jnp.sum(side_raw * side_raw, axis=0))), 1.0)
    axis_one = side_raw / side_len
    axis_two = cross_rows(normal, axis_one)
    relative = corner - centre[:, None]
    local_x = lax.optimization_barrier(jnp.sum(relative * axis_one[:, None], axis=0))
    local_y = lax.optimization_barrier(jnp.sum(relative * axis_two[:, None], axis=0))
    vel_x = lax.optimization_barrier(jnp.sum(corner_vel * axis_one[:, None], axis=0))
    vel_y = lax.optimization_barrier(jnp.sum(corner_vel * axis_two[:, None], axis=0))
    deriv_x = jnp.stack([local_y[1] - local_y[3], local_y[2] - local_y[0], local_y[3] - local_y[1], local_y[0] - local_y[2]]) / twice_area
    deriv_y = jnp.stack([local_x[3] - local_x[1], local_x[0] - local_x[2], local_x[1] - local_x[3], local_x[2] - local_x[0]]) / twice_area
    rate_xx = lax.optimization_barrier(jnp.sum(deriv_x * vel_x, axis=0))
    rate_yy = lax.optimization_barrier(jnp.sum(deriv_y * vel_y, axis=0))
    rate_xy = lax.optimization_barrier(jnp.sum(deriv_y * vel_x + deriv_x * vel_y, axis=0))
    plane_stiff = YOUNG / (1.0 - POISSON * POISSON)
    stress_new = stress_now + TIME_STEP * jnp.stack([plane_stiff * (rate_xx + POISSON * rate_yy), plane_stiff * (POISSON * rate_xx + rate_yy), YOUNG / (2.0 * (1.0 + POISSON)) * rate_xy])
    half_area = 0.5 * twice_area
    force_x = half_area * (deriv_x * stress_new[0] + deriv_y * stress_new[2])
    force_y = half_area * (deriv_y * stress_new[1] + deriv_x * stress_new[2])
    hour_signs = jnp.array(HOUR_SIGNS, jnp.float32)[:, None]
    hour_x = lax.optimization_barrier(jnp.sum(hour_signs * local_x, axis=0))
    hour_y = lax.optimization_barrier(jnp.sum(hour_signs * local_y, axis=0))
    hour_shape = hour_signs - hour_x * deriv_x - hour_y * deriv_y
    hour_rate = lax.optimization_barrier(jnp.sum(hour_shape[None] * corner_vel, axis=1))
    internal = force_x[None] * axis_one[:, None] + force_y[None] * axis_two[:, None] + HOURGLASS * hour_shape[None] * hour_rate[:, None]
    return (internal, stress_new, centre, normal)

def contact_tiles(slaves, candidates, live_mask):
    centre = candidates[:, :, 0:3]
    normal = candidates[:, :, 3:6]
    offset = slaves[None, :, :, :, None] - centre[:, :, :, None, :]
    gap_depth = lax.optimization_barrier(jnp.sum(offset * normal[:, :, :, None, :], axis=2))
    spread = lax.optimization_barrier(jnp.sum(offset * offset, axis=2)) - gap_depth * gap_depth
    weight = PENALTY * jnp.maximum(-gap_depth, 0.0) * jnp.exp(-spread / REACH) * live_mask[:, :, :, None]
    slave_force = jnp.einsum('kgij,kgcj->gci', weight, normal, precision=HIGH)
    reaction = -normal * lax.optimization_barrier(jnp.sum(weight, axis=2))[:, :, None, :]
    return (slave_force, reaction)

def roll_devices(values_in, amount, axis_pos):
    shaped = values_in.reshape((N_MESH, N_SUB) + values_in.shape[1:])
    return jnp.roll(shaped, amount, axis=axis_pos).reshape(values_in.shape)

def swap_peers(values_in):
    shaped = values_in.reshape((N_MESH, N_SUB, N_MESH, CAP) + values_in.shape[2:])
    order = (2, 1, 0, 3) + tuple(range(4, shaped.ndim))
    return shaped.transpose(order).reshape(values_in.shape)

def reference(coords, veloc, node_mass, stress, connect, send_mesh, send_sub, send_pick, bucket_list, pair_mask):
    devices = N_MESH * N_SUB
    total_nodes = NODE_DEV + GHOST_M + GHOST_S
    bucket_count = NODE_DEV // SEG
    block_count = ELEM_DEV // SEG
    positions = coords.reshape(3, devices, NODE_DEV).transpose(1, 0, 2)
    velocity = veloc.reshape(3, devices, NODE_DEV).transpose(1, 0, 2)
    masses = node_mass.reshape(devices, NODE_DEV)
    stress_now = stress.reshape(3, devices, ELEM_DEV).transpose(1, 0, 2)
    elem_nodes = connect.reshape(4, devices, ELEM_DEV).transpose(1, 0, 2)
    mesh_lists = send_mesh.reshape(devices, GHOST_M)
    sub_lists = send_sub.reshape(devices, GHOST_S)
    picks_all = send_pick.reshape(STEPS, devices, SLOTS)
    lists_all = bucket_list.reshape(STEPS, CAND, devices, bucket_count).transpose(0, 2, 1, 3)
    masks_all = pair_mask.reshape(STEPS, CAND, devices, NODE_DEV).transpose(0, 2, 1, 3).astype(jnp.float32)
    slot_ids = jnp.arange(SLOTS, dtype=jnp.int32)
    block_ids = jnp.arange(block_count, dtype=jnp.int32)
    take_cols = jax.vmap(lambda source, column_ids: source[:, column_ids])
    take_rows = jax.vmap(lambda source, row_ids: source[row_ids])
    add_cols = jax.vmap(lambda target, column_ids, extra_force: target.at[:, column_ids].add(extra_force))
    scatter_cols = jax.vmap(lambda forces_in, column_ids: jnp.zeros((3, total_nodes), jnp.float32).at[:, column_ids].add(forces_in))

    def one_device(device_items):
        own_pos, slot_geo, cand_lists, live_mask = device_items
        slave_rows = own_pos.reshape(3, bucket_count, SEG).transpose(1, 0, 2)
        slave_force, reaction = contact_tiles(slave_rows, slot_geo[cand_lists], live_mask.reshape(CAND, bucket_count, SEG))
        onehot = (cand_lists.reshape(-1)[:, None] == slot_ids[None, :]).astype(jnp.float32)
        slot_react = jnp.dot(onehot.T, reaction.reshape(CAND * bucket_count, 3 * SEG), precision=HIGH)
        return (slave_force.transpose(1, 0, 2).reshape(3, NODE_DEV), slot_react.reshape(SLOTS, 3, SEG))
    for step_index in range(STEPS):
        packed = jnp.concatenate([positions, velocity], axis=1)
        from_mesh = roll_devices(take_cols(packed, mesh_lists), 1, 0)
        from_sub = roll_devices(take_cols(packed, sub_lists), 1, 1)
        pos_table = jnp.concatenate([positions, from_mesh[:, 0:3], from_sub[:, 0:3]], axis=2)
        vel_table = jnp.concatenate([velocity, from_mesh[:, 3:6], from_sub[:, 3:6]], axis=2)
        corner = take_cols(pos_table, elem_nodes)
        corner_vel = take_cols(vel_table, elem_nodes)
        internal, stress_now, centre, normal = jax.vmap(shell_forces)(corner, corner_vel, stress_now)
        geometry_blocks = jnp.concatenate([centre, normal], axis=1).reshape(devices, 6, block_count, SEG).transpose(0, 2, 1, 3)
        outgoing = take_rows(geometry_blocks, picks_all[step_index])
        incoming = swap_peers(outgoing)
        slave_force, slot_react = lax.map(one_device, (positions, incoming, lists_all[step_index], masks_all[step_index]))
        returned = swap_peers(slot_react).reshape(devices, SLOTS, 3 * SEG)
        pick_hot = (picks_all[step_index][:, :, None] == block_ids[None, None, :]).astype(jnp.float32)
        seg_react = jnp.einsum('dqb,dqx->dbx', pick_hot, returned, precision=HIGH)
        seg_react = seg_react.reshape(devices, block_count, 3, SEG).transpose(0, 2, 1, 3).reshape(devices, 3, ELEM_DEV)
        elem_force = 0.25 * seg_react[:, :, None, :] - internal
        node_force = scatter_cols(elem_force, elem_nodes)
        back_mesh = roll_devices(node_force[:, :, NODE_DEV:NODE_DEV + GHOST_M], -1, 0)
        back_sub = roll_devices(node_force[:, :, NODE_DEV + GHOST_M:], -1, 1)
        own_force = add_cols(add_cols(node_force[:, :, :NODE_DEV], mesh_lists, back_mesh), sub_lists, back_sub)
        velocity = velocity + TIME_STEP * (own_force + slave_force) / masses[:, None, :]
        positions = positions + TIME_STEP * velocity
    return (velocity.transpose(1, 0, 2).reshape(3, devices * NODE_DEV), stress_now.transpose(1, 0, 2).reshape(3, devices * ELEM_DEV))
```

```python
import functools
import math

import jax
import jax.numpy as jnp
from jax import lax
from jax.experimental import pallas as pl
from jax.experimental.pallas import tpu as pltpu
from jax.sharding import PartitionSpec as P

SEG = 128
STEPS = 4
LOW = 256
ROWS = 8

TIME_STEP = 0.2
YOUNG = 1.0
POISSON = 0.3
HOURGLASS = 0.01
PENALTY = 0.2
REACH = 4.0
HOUR_SIGNS = (1.0, -1.0, 1.0, -1.0)

F32 = jnp.float32
BF16 = jnp.bfloat16


def shifted(value, axis, steps):
    count = lax.axis_size(axis)
    pairs = [(source, (source + steps) % count) for source in range(count)]
    return lax.ppermute(value, axis, pairs)


def split_two(value):
    high = value.astype(BF16).astype(F32)
    return high, value - high


def split_three(value):
    high = value.astype(BF16).astype(F32)
    rest = value - high
    mid = rest.astype(BF16).astype(F32)
    return high, mid, rest - mid


def one_hot_low(low_ids):
    width = low_ids.shape[1]
    rows = lax.broadcasted_iota(jnp.int32, (LOW, width), 0)
    return jnp.where(rows == low_ids, 1.0, 0.0).astype(BF16)


def stack_columns(rows_eight):
    count = rows_eight.shape[1] // LOW
    return jnp.concatenate(
        [rows_eight[:, part * LOW : (part + 1) * LOW] for part in range(count)], axis=0
    )


def pick_high(product, high_ids, count):
    width = product.shape[1]
    total = jnp.zeros((ROWS, width), F32)
    for part in range(count):
        total = jnp.where(high_ids == part, product[part * ROWS : (part + 1) * ROWS], total)
    return total


def split_rows(three):
    high, low = split_two(three)
    pad = jnp.zeros((ROWS - 6, three.shape[1]), F32)
    return jnp.concatenate([high, low, pad], axis=0)


def gather_tiles(table, conn_ref, out_ref):
    count = table.shape[0] // ROWS

    def tile(index, carry):
        ids = conn_ref[pl.ds(index, 1), :]
        product = jnp.dot(table, one_hot_low(ids & (LOW - 1)), preferred_element_type=F32)
        total = pick_high(product, ids >> 8, count)
        for half in range(LOW // SEG):
            start = pl.multiple_of((index * (LOW // SEG) + half) * ROWS, ROWS)
            out_ref[pl.ds(start, ROWS), :] = total[:, half * SEG : (half + 1) * SEG]
        return carry

    lax.fori_loop(0, conn_ref.shape[0], tile, 0, unroll=4)


def cross(left, right):
    return (
        left[1] * right[2] - left[2] * right[1],
        left[2] * right[0] - left[0] * right[2],
        left[0] * right[1] - left[1] * right[0],
    )


def sub3(left, right):
    return tuple(a - b for a, b in zip(left, right))


def dot3(left, right):
    return left[0] * right[0] + left[1] * right[1] + left[2] * right[2]


def geometry(corner):
    raw = cross(sub3(corner[2], corner[0]), sub3(corner[3], corner[1]))
    twice_area = jnp.maximum(jnp.sqrt(dot3(raw, raw)), 1.0)
    inverse = 1.0 / twice_area
    normal = tuple(part * inverse for part in raw)
    centre = tuple(
        0.25 * (corner[0][c] + corner[1][c] + corner[2][c] + corner[3][c]) for c in range(3)
    )
    return centre, normal, twice_area, inverse


def corner_rows(ref, blocks, group, component):
    return [
        ref[pl.ds((corner * blocks + group * 8) * ROWS + component, 8, stride=ROWS), :]
        for corner in range(4)
    ]


def geometry_kernel(
    picks_ref, own_ref, mesh_ref, sub_ref, conn_ref, corner_ref, geo_ref, out_ref, rows_ref
):
    blocks = geo_ref.shape[0] // ROWS
    full = jnp.concatenate([own_ref[0:3, :], mesh_ref[0:3, :], sub_ref[0:3, :]], axis=1)
    gather_tiles(stack_columns(split_rows(full)).astype(BF16), conn_ref, rows_ref)
    for group in range(blocks // 8):
        parts = []
        for component in range(3):
            high = corner_rows(rows_ref, blocks, group, component)
            low = corner_rows(rows_ref, blocks, group, component + 3)
            parts.append([a + b for a, b in zip(high, low)])
        corner = [tuple(parts[c][i] for c in range(3)) for i in range(4)]
        for i in range(4):
            for c in range(3):
                corner_ref[i * 3 + c, group * 8 : (group + 1) * 8, :] = corner[i][c]
        centre, normal, _, _ = geometry(corner)
        for c in range(3):
            geo_ref[pl.ds(group * 8 * ROWS + c, 8, stride=ROWS), :] = centre[c]
            geo_ref[pl.ds(group * 8 * ROWS + 3 + c, 8, stride=ROWS), :] = normal[c]
        for c in range(6, ROWS):
            geo_ref[pl.ds(group * 8 * ROWS + c, 8, stride=ROWS), :] = jnp.zeros((8, SEG), F32)
    for slot in range(out_ref.shape[0] // ROWS):
        start = pl.multiple_of(picks_ref[slot] * ROWS, ROWS)
        out_ref[slot * ROWS : (slot + 1) * ROWS, :] = geo_ref[pl.ds(start, ROWS), :]


def force_kernel(
    own_ref, mesh_ref, sub_ref, conn_ref, corner_ref, stress_ref, internal_ref, new_ref, rows_ref
):
    blocks = corner_ref.shape[1]
    full = jnp.concatenate([own_ref[3:6, :], mesh_ref[3:6, :], sub_ref[3:6, :]], axis=1)
    gather_tiles(stack_columns(split_rows(full)).astype(BF16), conn_ref, rows_ref)
    stiff = YOUNG / (1.0 - POISSON * POISSON)
    for group in range(blocks // 8):
        here = slice(group * 8, (group + 1) * 8)
        speed_parts = []
        for component in range(3):
            high = corner_rows(rows_ref, blocks, group, component)
            low = corner_rows(rows_ref, blocks, group, component + 3)
            speed_parts.append([a + b for a, b in zip(high, low)])
        speed = [tuple(speed_parts[c][i] for c in range(3)) for i in range(4)]
        corner = [tuple(corner_ref[i * 3 + c, here, :] for c in range(3)) for i in range(4)]
        centre, normal, twice_area, inverse = geometry(corner)
        side = sub3(corner[1], corner[0])
        side_inverse = 1.0 / jnp.maximum(jnp.sqrt(dot3(side, side)), 1.0)
        axis_one = tuple(part * side_inverse for part in side)
        axis_two = cross(normal, axis_one)
        relative = [sub3(corner[i], centre) for i in range(4)]
        x = [dot3(relative[i], axis_one) for i in range(4)]
        y = [dot3(relative[i], axis_two) for i in range(4)]
        u = [dot3(speed[i], axis_one) for i in range(4)]
        v = [dot3(speed[i], axis_two) for i in range(4)]
        y13, y20 = (y[1] - y[3]) * inverse, (y[2] - y[0]) * inverse
        x31, x02 = (x[3] - x[1]) * inverse, (x[0] - x[2]) * inverse
        bx = [y13, y20, -y13, -y20]
        by = [x31, x02, -x31, -x02]
        u02, u13, v02, v13 = u[0] - u[2], u[1] - u[3], v[0] - v[2], v[1] - v[3]
        rate_xx = y13 * u02 + y20 * u13
        rate_yy = x31 * v02 + x02 * v13
        rate_xy = x31 * u02 + x02 * u13 + y13 * v02 + y20 * v13
        s0 = stress_ref[0, here, :] + TIME_STEP * (stiff * (rate_xx + POISSON * rate_yy))
        s1 = stress_ref[1, here, :] + TIME_STEP * (stiff * (POISSON * rate_xx + rate_yy))
        s2 = stress_ref[2, here, :] + TIME_STEP * (YOUNG / (2.0 * (1.0 + POISSON)) * rate_xy)
        new_ref[0, here, :] = s0
        new_ref[1, here, :] = s1
        new_ref[2, here, :] = s2
        half_area = 0.5 * twice_area
        hour_x = x[0] - x[1] + x[2] - x[3]
        hour_y = y[0] - y[1] + y[2] - y[3]
        shape = [HOUR_SIGNS[i] - hour_x * bx[i] - hour_y * by[i] for i in range(4)]
        rate = tuple(
            HOURGLASS * sum(shape[i] * speed[i][c] for i in range(4)) for c in range(3)
        )
        for i in range(4):
            force_x = half_area * (bx[i] * s0 + by[i] * s2)
            force_y = half_area * (by[i] * s1 + bx[i] * s2)
            for c in range(3):
                internal_ref[i * 3 + c, here, :] = (
                    force_x * axis_one[c] + force_y * axis_two[c] + shape[i] * rate[c]
                )


def contact_kernel(list_ref, own_ref, slots_ref, mask_ref, force_ref, react_ref):
    buckets = own_ref.shape[1] // SEG
    cands = mask_ref.shape[0]
    scale = math.sqrt(math.log2(math.e) / REACH)
    react_ref[...] = jnp.zeros_like(react_ref)

    def bucket(index, carry):
        start = pl.multiple_of(index * SEG, SEG)
        own = own_ref[0:3, pl.ds(start, SEG)] * scale
        mask = mask_ref[:, pl.ds(start, SEG)].astype(F32) * (-PENALTY / scale)
        pad = jnp.zeros((ROWS - 3 - cands, SEG), F32)
        turned = jnp.concatenate([own, mask, pad], axis=0).T
        slots, segs = [], []
        for k in range(cands):
            slot = list_ref[k, index]
            slots.append(slot)
            tile = slots_ref[pl.ds(pl.multiple_of(slot * ROWS, ROWS), ROWS), :]
            segs.append(
                [jnp.broadcast_to(tile[c : c + 1] * scale, (8, SEG)) for c in range(3)]
                + [jnp.broadcast_to(tile[c : c + 1], (8, SEG)) for c in range(3, 6)]
            )
        sums = [jnp.zeros((8, SEG), F32) for _ in range(cands)]
        columns = [[], [], []]
        for group in range(SEG // 8):
            node = turned[group * 8 : (group + 1) * 8]
            place = [jnp.broadcast_to(node[:, c : c + 1], (8, SEG)) for c in range(3)]
            total = [None, None, None]
            for k in range(cands):
                centre, normal = segs[k][0:3], segs[k][3:6]
                offset = [place[c] - centre[c] for c in range(3)]
                gap = dot3(offset, normal)
                power = gap * gap - dot3(offset, offset)
                weight = (
                    jnp.minimum(gap, 0.0)
                    * jnp.exp2(power)
                    * jnp.broadcast_to(node[:, 3 + k : 4 + k], (8, SEG))
                )
                sums[k] = sums[k] + weight
                for c in range(3):
                    part = weight * normal[c]
                    total[c] = part if total[c] is None else total[c] + part
            for c in range(3):
                columns[c].append(jnp.sum(total[c], axis=1, keepdims=True))
        cols = [jnp.concatenate(columns[c], axis=0) for c in range(3)]
        block = jnp.concatenate(cols + [jnp.zeros((SEG, ROWS - 3), F32)], axis=1)
        force_ref[:, pl.ds(start, SEG)] = block.T
        for k in range(cands):
            react_ref[pl.ds(slots[k], 1), :] += jnp.sum(sums[k], axis=0, keepdims=True)
        return carry

    lax.fori_loop(0, buckets, bucket, 0)


def scatter_kernel(
    picks_ref, internal_ref, geo_ref, back_ref, conn_ref, own_ref, mesh_ref, sub_ref,
    seg_ref, rows_ref, acc_ref,
):
    blocks = internal_ref.shape[1]
    seg_ref[...] = jnp.zeros_like(seg_ref)
    for slot in range(back_ref.shape[0]):
        seg_ref[pl.ds(picks_ref[slot], 1), :] += back_ref[slot : slot + 1, :]
    for group in range(blocks // 8):
        here = slice(group * 8, (group + 1) * 8)
        react = -0.25 * seg_ref[here, :]
        for c in range(3):
            push = react * geo_ref[pl.ds(group * 8 * ROWS + 3 + c, 8, stride=ROWS), :]
            for i in range(4):
                high, low = split_two(push - internal_ref[i * 3 + c, here, :])
                start = (i * blocks + group * 8) * ROWS
                rows_ref[pl.ds(start + c, 8, stride=ROWS), :] = high
                rows_ref[pl.ds(start + 3 + c, 8, stride=ROWS), :] = low
    for i in range(4):
        for group in range(blocks // 8):
            start = (i * blocks + group * 8) * ROWS
            for c in range(6, ROWS):
                rows_ref[pl.ds(start + c, 8, stride=ROWS), :] = jnp.zeros((8, SEG), F32)
    scatter_tiles(rows_ref, conn_ref, acc_ref)
    full = unstack(acc_ref, 0, acc_ref.shape[0] // ROWS)
    first = own_ref.shape[1]
    second = first + mesh_ref.shape[1]
    own_ref[...] = full[:, :first]
    mesh_ref[...] = full[:, first:second]
    sub_ref[...] = full[:, second:]


def scatter_tiles(rows_ref, conn_ref, acc_ref):
    count = acc_ref.shape[0] // ROWS
    acc_ref[...] = jnp.zeros_like(acc_ref)

    def tile(index, carry):
        ids = conn_ref[pl.ds(index, 1), :]
        start = pl.multiple_of(index * (LOW // SEG) * ROWS, ROWS * (LOW // SEG))
        parts = [rows_ref[pl.ds(start + half * ROWS, ROWS), :] for half in range(LOW // SEG)]
        values = jnp.concatenate(parts, axis=1)
        high_ids = ids >> 8
        spread = jnp.concatenate(
            [jnp.where(high_ids == part, values, 0.0) for part in range(count)], axis=0
        ).astype(BF16)
        acc_ref[...] += lax.dot_general(
            spread,
            one_hot_low(ids & (LOW - 1)),
            (((1,), (1,)), ((), ())),
            preferred_element_type=F32,
        )
        return carry

    lax.fori_loop(0, conn_ref.shape[0], tile, 0, unroll=4)


def unstack(acc_ref, first, last):
    parts = [acc_ref[part * ROWS : (part + 1) * ROWS, :] for part in range(first, last)]
    full = jnp.concatenate(parts, axis=1)
    total = full[0:3] + full[3:6]
    return jnp.concatenate([total, jnp.zeros((ROWS - 3, total.shape[1]), F32)], axis=0)


def add_back(back, ids_ref, count):
    total = jnp.zeros((count * ROWS, LOW), F32)
    high, low = split_two(back[0:3])
    pad = jnp.zeros((ROWS - 6, back.shape[1]), F32)
    rows = jnp.concatenate([high, low, pad], axis=0)
    for index in range(ids_ref.shape[0]):
        ids = ids_ref[index : index + 1, :]
        values = rows[:, index * LOW : (index + 1) * LOW]
        spread = jnp.concatenate(
            [jnp.where((ids >> 8) == part, values, 0.0) for part in range(count)], axis=0
        ).astype(BF16)
        total = total + lax.dot_general(
            spread,
            one_hot_low(ids & (LOW - 1)),
            (((1,), (1,)), ((), ())),
            preferred_element_type=F32,
        )
    return total


def pack_ghosts(own, ids_ref, out_ref):
    count = own.shape[1] // LOW
    tables = [stack_columns(part).astype(BF16) for part in split_three(own)]
    for index in range(ids_ref.shape[0]):
        ids = ids_ref[index : index + 1, :]
        hot = one_hot_low(ids & (LOW - 1))
        product = sum(jnp.dot(table, hot, preferred_element_type=F32) for table in tables)
        out_ref[:, index * LOW : (index + 1) * LOW] = pick_high(product, ids >> 8, count)


def pack_kernel(own_ref, mesh_ids_ref, sub_ids_ref, to_mesh_ref, to_sub_ref):
    own = own_ref[...]
    pack_ghosts(own, mesh_ids_ref, to_mesh_ref)
    pack_ghosts(own, sub_ids_ref, to_sub_ref)


def update_kernel(
    own_ref, force_ref, slave_ref, back_mesh_ref, back_sub_ref, mass_ref, mesh_ids_ref,
    sub_ids_ref, new_ref, to_mesh_ref, to_sub_ref,
):
    count = own_ref.shape[1] // LOW
    extra = add_back(back_mesh_ref[...], mesh_ids_ref, count) + add_back(
        back_sub_ref[...], sub_ids_ref, count
    )
    full = jnp.concatenate(
        [extra[part * ROWS : (part + 1) * ROWS] for part in range(count)], axis=1
    )
    force = force_ref[0:3, :] + slave_ref[0:3, :] + (full[0:3] + full[3:6])
    speed = own_ref[3:6, :] + TIME_STEP * force / mass_ref[...]
    place = own_ref[0:3, :] + TIME_STEP * speed
    own = jnp.concatenate([place, speed, jnp.zeros((ROWS - 6, place.shape[1]), F32)], axis=0)
    new_ref[...] = own
    if to_mesh_ref is not None:
        pack_ghosts(own, mesh_ids_ref, to_mesh_ref)
        pack_ghosts(own, sub_ids_ref, to_sub_ref)


def last_kernel(*refs):
    update_kernel(*refs, None, None)


VM = pl.BlockSpec(memory_space=pltpu.VMEM)
SM = pl.BlockSpec(memory_space=pltpu.SMEM)


def call(kernel, outs, ins, scratch=(), name=None, flops=0):
    shapes = tuple(jax.ShapeDtypeStruct(shape, F32) for shape in outs)
    return pl.pallas_call(
        kernel,
        out_shape=shapes,
        in_specs=list(ins),
        out_specs=tuple(VM for _ in outs),
        scratch_shapes=[pltpu.VMEM(shape, F32) for shape in scratch],
        name=name,
        cost_estimate=pl.CostEstimate(flops=flops, bytes_accessed=1 << 20, transcendentals=0),
    )


def per_device(
    coords,
    veloc,
    node_mass,
    stress,
    connect,
    send_mesh,
    send_sub,
    send_pick,
    bucket_list,
    pair_mask,
):
    nodes = coords.shape[1]
    elems = stress.shape[1]
    ghost_mesh = send_mesh.shape[0]
    ghost_sub = send_sub.shape[0]
    width = nodes + ghost_mesh + ghost_sub
    peers = lax.axis_size("mesh")
    slots = send_pick.shape[1]
    per_peer = slots // peers
    blocks = elems // SEG
    conn = connect.reshape(4 * elems // LOW, LOW)
    mesh_ids = send_mesh.reshape(ghost_mesh // LOW, LOW)
    sub_ids = send_sub.reshape(ghost_sub // LOW, LOW)
    mass = node_mass.reshape(1, nodes)
    stress_now = stress.reshape(3, blocks, SEG)
    own = jnp.concatenate([coords, veloc, jnp.zeros((ROWS - 6, nodes), F32)], axis=0)

    pack = call(pack_kernel, [(ROWS, ghost_mesh), (ROWS, ghost_sub)], [VM] * 3, name="pack")
    geom = call(
        geometry_kernel,
        [(12, blocks, SEG), (blocks * ROWS, SEG), (slots * ROWS, SEG)],
        [SM] + [VM] * 4,
        [(4 * blocks * ROWS, SEG)],
        name="geometry",
        flops=1 << 30,
    )
    forces = call(
        force_kernel,
        [(12, blocks, SEG), (3, blocks, SEG)],
        [VM] * 6,
        [(4 * blocks * ROWS, SEG)],
        name="forces",
        flops=1 << 31,
    )
    contact = call(
        contact_kernel, [(ROWS, nodes), (slots, SEG)], [SM] + [VM] * 3, name="contact",
        flops=1 << 31,
    )
    scatter = call(
        scatter_kernel,
        [(ROWS, nodes), (ROWS, ghost_mesh), (ROWS, ghost_sub)],
        [SM] + [VM] * 4,
        [(blocks, SEG), (4 * blocks * ROWS, SEG), (width // LOW * ROWS, LOW)],
        name="scatter",
        flops=1 << 30,
    )
    update = call(
        update_kernel,
        [(ROWS, nodes), (ROWS, ghost_mesh), (ROWS, ghost_sub)],
        [VM] * 8,
        name="update",
    )
    finish = call(last_kernel, [(ROWS, nodes)], [VM] * 8, name="finish")

    to_mesh, to_sub = pack(own, mesh_ids, sub_ids)
    for step in range(STEPS):
        from_mesh = shifted(to_mesh, "mesh", 1)
        from_sub = shifted(to_sub, "sub", 1)
        picks = send_pick[step]
        corner, geo, outgoing = geom(picks, own, from_mesh, from_sub, conn)
        incoming = lax.all_to_all(
            outgoing.reshape(peers, per_peer * ROWS, SEG),
            "mesh", split_axis=0, concat_axis=0, tiled=True,
        ).reshape(slots * ROWS, SEG)
        internal, stress_now = forces(own, from_mesh, from_sub, conn, corner, stress_now)
        slave, react = contact(bucket_list[step], own, incoming, pair_mask[step])
        returned = lax.all_to_all(
            react.reshape(peers, per_peer, SEG),
            "mesh", split_axis=0, concat_axis=0, tiled=True,
        ).reshape(slots, SEG)
        force, back_mesh, back_sub = scatter(picks, internal, geo, returned, conn)
        back_mesh = shifted(back_mesh, "mesh", -1)
        back_sub = shifted(back_sub, "sub", -1)
        args = (own, force, slave, back_mesh, back_sub, mass, mesh_ids, sub_ids)
        if step < STEPS - 1:
            own, to_mesh, to_sub = update(*args)
        else:
            (own,) = finish(*args)
    return own[3:6], stress_now.reshape(3, elems)


def solution(mesh):
    return jax.shard_map(
        per_device,
        mesh=mesh,
        in_specs=(
            P(None, ("mesh", "sub")),
            P(None, ("mesh", "sub")),
            P(("mesh", "sub")),
            P(None, ("mesh", "sub")),
            P(None, ("mesh", "sub")),
            P(("mesh", "sub")),
            P(("mesh", "sub")),
            P(None, ("mesh", "sub")),
            P(None, None, ("mesh", "sub")),
            P(None, None, ("mesh", "sub")),
        ),
        out_specs=(P(None, ("mesh", "sub")), P(None, ("mesh", "sub"))),
        check_vma=False,
    )
```

```python
import functools
import math

import jax
import jax.numpy as jnp
from jax import lax
from jax.experimental import pallas as pl
from jax.experimental.pallas import tpu as pltpu
from jax.sharding import PartitionSpec as P


SEG = 128
STEPS = 4
LOW = 256
ROWS = 8
UNROLL = 16

TIME_STEP = 0.2
YOUNG = 1.0
POISSON = 0.3
HOURGLASS = 0.01
PENALTY = 0.2
REACH = 4.0
HOUR_SIGNS = (1.0, -1.0, 1.0, -1.0)

F32 = jnp.float32
BF16 = jnp.bfloat16


def shifted(value, axis, steps):
    count = lax.axis_size(axis)
    pairs = [(source, (source + steps) % count) for source in range(count)]
    return lax.ppermute(value, axis, pairs)


def split_two(value):
    high = value.astype(BF16).astype(F32)
    return high, value - high


def split_three(value):
    high = value.astype(BF16).astype(F32)
    rest = value - high
    mid = rest.astype(BF16).astype(F32)
    return high, mid, rest - mid


def one_hot_low(low_ids):
    width = low_ids.shape[1]
    rows = lax.broadcasted_iota(jnp.int32, (LOW, width), 0)
    return jnp.where(rows == low_ids, 1.0, 0.0).astype(BF16)


def stack_columns(rows_eight):
    count = rows_eight.shape[1] // LOW
    return jnp.concatenate(
        [rows_eight[:, part * LOW : (part + 1) * LOW] for part in range(count)], axis=0
    )


def pick_high(product, high_ids, count):
    width = product.shape[1]
    total = jnp.zeros((ROWS, width), F32)
    for part in range(count):
        total = jnp.where(high_ids == part, product[part * ROWS : (part + 1) * ROWS], total)
    return total


def split_rows(three):
    high, low = split_two(three)
    pad = jnp.zeros((ROWS - 6, three.shape[1]), F32)
    return jnp.concatenate([high, low, pad], axis=0)


def gather_tiles(table, conn_ref, out_ref):
    count = table.shape[0] // ROWS

    def tile(index, carry):
        ids = conn_ref[pl.ds(index, 1), :]
        product = jnp.dot(table, one_hot_low(ids & (LOW - 1)), preferred_element_type=F32)
        total = pick_high(product, ids >> 8, count)
        for half in range(LOW // SEG):
            start = pl.multiple_of((index * (LOW // SEG) + half) * ROWS, ROWS)
            out_ref[pl.ds(start, ROWS), :] = total[:, half * SEG : (half + 1) * SEG]
        return carry

    lax.fori_loop(0, conn_ref.shape[0], tile, 0, unroll=UNROLL)


def cross(left, right):
    return (
        left[1] * right[2] - left[2] * right[1],
        left[2] * right[0] - left[0] * right[2],
        left[0] * right[1] - left[1] * right[0],
    )


def sub3(left, right):
    return tuple(a - b for a, b in zip(left, right))


def dot3(left, right):
    return left[0] * right[0] + left[1] * right[1] + left[2] * right[2]


def geometry(corner):
    raw = cross(sub3(corner[2], corner[0]), sub3(corner[3], corner[1]))
    twice_area = jnp.maximum(jnp.sqrt(dot3(raw, raw)), 1.0)
    inverse = 1.0 / twice_area
    normal = tuple(part * inverse for part in raw)
    centre = tuple(
        0.25 * (corner[0][c] + corner[1][c] + corner[2][c] + corner[3][c]) for c in range(3)
    )
    return centre, normal, twice_area, inverse


def corner_rows(ref, group, component):
    return [
        ref[pl.ds((group * 32 + corner) * ROWS + component, 8, stride=4 * ROWS), :]
        for corner in range(4)
    ]


def tree_pick(values, bits):
    level = 0
    while len(values) > 1:
        values = [
            jnp.where(bits[level], values[i + 1], values[i]) if i + 1 < len(values) else values[i]
            for i in range(0, len(values), 2)
        ]
        level += 1
    return values[0]


def fill_chunks(three, chunk_ref, first):
    four = jnp.concatenate([three, jnp.zeros((1, three.shape[1]), F32)], axis=0)
    twice = jnp.concatenate([four, four], axis=0)
    for part in range(three.shape[1] // SEG):
        chunk_ref[first + part] = twice[:, part * SEG : (part + 1) * SEG]


def lane_ids(conn_ref, index):
    ids = conn_ref[pl.ds(index, 1), :]
    halves = [jnp.broadcast_to(ids[:, h * SEG : (h + 1) * SEG], (4, SEG)) for h in range(2)]
    return jnp.concatenate(halves, axis=0)


def lane_pick(chunk_ref, ids, high_ids):
    count = chunk_ref.shape[0]
    low_ids = ids & (SEG - 1)
    bits = [((high_ids >> bit) & 1) == 1 for bit in range((count - 1).bit_length())]
    values = [
        jnp.take_along_axis(chunk_ref[part], low_ids, axis=1, mode="promise_in_bounds")
        for part in range(count)
    ]
    return tree_pick(values, bits)


def own_rows_kernel(own_ref, conn_ref, rows_ref, chunk_ref):
    fill_chunks(own_ref[0:3, :], chunk_ref, 0)

    def tile(index, carry):
        ids = lane_ids(conn_ref, index)
        start = pl.multiple_of(index * ROWS, ROWS)
        rows_ref[pl.ds(start, ROWS), :] = lane_pick(chunk_ref, ids, ids >> 7)
        return carry

    lax.fori_loop(0, conn_ref.shape[0], tile, 0, unroll=8)


def geometry_kernel(
    step, nodes, picks_any, mesh_ref, sub_ref, conn_ref, own_rows_ref, corner_ref, geo_ref,
    out_ref, kept_ref, rows_ref, chunk_ref, picks_ref, sem,
):
    fetch = pltpu.make_async_copy(picks_any, picks_ref, sem)
    fetch.start()
    blocks = geo_ref.shape[0] // ROWS
    first = mesh_ref.shape[1] // SEG
    fill_chunks(mesh_ref[0:3, :], chunk_ref, 0)
    fill_chunks(sub_ref[0:3, :], chunk_ref, first)

    def tile(index, carry):
        ids = lane_ids(conn_ref, index)
        start = pl.multiple_of(index * ROWS, ROWS)
        far = lane_pick(chunk_ref, ids, (ids >> 7) - nodes // SEG)
        near = own_rows_ref[pl.ds(start, ROWS), :]
        rows_ref[pl.ds(start, ROWS), :] = jnp.where(ids >= nodes, far, near)
        return carry

    lax.fori_loop(0, conn_ref.shape[0], tile, 0, unroll=16)
    for group in range(blocks // 8):
        corner = [
            tuple(rows_ref[pl.ds(group * 128 + i * 4 + c, 8, stride=16), :] for c in range(3))
            for i in range(4)
        ]
        for i in range(4):
            for c in range(3):
                corner_ref[i * 3 + c, group * 8 : (group + 1) * 8, :] = corner[i][c]
        centre, normal, _, _ = geometry(corner)
        for c in range(3):
            geo_ref[pl.ds(group * 8 * ROWS + c, 8, stride=ROWS), :] = centre[c]
            geo_ref[pl.ds(group * 8 * ROWS + 3 + c, 8, stride=ROWS), :] = normal[c]
        for c in range(6, ROWS):
            geo_ref[pl.ds(group * 8 * ROWS + c, 8, stride=ROWS), :] = jnp.zeros((8, SEG), F32)

    def copy(slot, carry):
        start = pl.multiple_of(picks_ref[step, slot] * ROWS, ROWS)
        here = pl.ds(pl.multiple_of(slot * ROWS, ROWS), ROWS)
        block = geo_ref[pl.ds(start, ROWS), :]
        out_ref[here, :] = block
        kept_ref[here, :] = block
        return carry

    fetch.wait()
    lax.fori_loop(0, out_ref.shape[0] // ROWS, copy, 0, unroll=16)


def force_kernel(
    own_ref, mesh_ref, sub_ref, conn_ref, corner_ref, stress_ref, push_ref, new_ref, rows_ref
):
    blocks = corner_ref.shape[1]
    full = jnp.concatenate([own_ref[3:6, :], mesh_ref[3:6, :], sub_ref[3:6, :]], axis=1)
    gather_tiles(stack_columns(split_rows(full)).astype(BF16), conn_ref, rows_ref)
    stiff = YOUNG / (1.0 - POISSON * POISSON)
    for group in range(blocks // 8):
        here = slice(group * 8, (group + 1) * 8)
        speed_parts = []
        for component in range(3):
            high = corner_rows(rows_ref, group, component)
            low = corner_rows(rows_ref, group, component + 3)
            speed_parts.append([a + b for a, b in zip(high, low)])
        speed = [tuple(speed_parts[c][i] for c in range(3)) for i in range(4)]
        corner = [tuple(corner_ref[i * 3 + c, here, :] for c in range(3)) for i in range(4)]
        centre, normal, twice_area, inverse = geometry(corner)
        side = sub3(corner[1], corner[0])
        side_inverse = 1.0 / jnp.maximum(jnp.sqrt(dot3(side, side)), 1.0)
        axis_one = tuple(part * side_inverse for part in side)
        axis_two = cross(normal, axis_one)
        relative = [sub3(corner[i], centre) for i in range(4)]
        x = [dot3(relative[i], axis_one) for i in range(4)]
        y = [dot3(relative[i], axis_two) for i in range(4)]
        u = [dot3(speed[i], axis_one) for i in range(4)]
        v = [dot3(speed[i], axis_two) for i in range(4)]
        y13, y20 = (y[1] - y[3]) * inverse, (y[2] - y[0]) * inverse
        x31, x02 = (x[3] - x[1]) * inverse, (x[0] - x[2]) * inverse
        bx = [y13, y20, -y13, -y20]
        by = [x31, x02, -x31, -x02]
        u02, u13, v02, v13 = u[0] - u[2], u[1] - u[3], v[0] - v[2], v[1] - v[3]
        rate_xx = y13 * u02 + y20 * u13
        rate_yy = x31 * v02 + x02 * v13
        rate_xy = x31 * u02 + x02 * u13 + y13 * v02 + y20 * v13
        s0 = stress_ref[0, here, :] + TIME_STEP * (stiff * (rate_xx + POISSON * rate_yy))
        s1 = stress_ref[1, here, :] + TIME_STEP * (stiff * (POISSON * rate_xx + rate_yy))
        s2 = stress_ref[2, here, :] + TIME_STEP * (YOUNG / (2.0 * (1.0 + POISSON)) * rate_xy)
        new_ref[0, here, :] = s0
        new_ref[1, here, :] = s1
        new_ref[2, here, :] = s2
        half_area = 0.5 * twice_area
        hour_x = x[0] - x[1] + x[2] - x[3]
        hour_y = y[0] - y[1] + y[2] - y[3]
        shape = [HOUR_SIGNS[i] - hour_x * bx[i] - hour_y * by[i] for i in range(4)]
        rate = tuple(
            HOURGLASS * sum(shape[i] * speed[i][c] for i in range(4)) for c in range(3)
        )
        for i in range(4):
            force_x = half_area * (bx[i] * s0 + by[i] * s2)
            force_y = half_area * (by[i] * s1 + bx[i] * s2)
            start = (group * 32 + i) * ROWS
            for c in range(3):
                internal = force_x * axis_one[c] + force_y * axis_two[c] + shape[i] * rate[c]
                high, low = split_two(-internal)
                push_ref[pl.ds(start + c, 8, stride=4 * ROWS), :] = high
                push_ref[pl.ds(start + 3 + c, 8, stride=4 * ROWS), :] = low
            for c in range(6, ROWS):
                push_ref[pl.ds(start + c, 8, stride=4 * ROWS), :] = jnp.zeros((8, SEG), F32)


def product_tiles(value, turn):
    parts = split_three(value)
    order = (0, 0, 1, 0, 1, 2) if turn else (0, 1, 0, 2, 1, 0)
    return [parts[index] for index in order]


def row_mix(three, extras):
    width = three.shape[1]
    rows = [three] + extras
    pad = ROWS - sum(part.shape[0] for part in rows)
    if pad:
        rows.append(jnp.zeros((pad, width), F32))
    return jnp.concatenate(rows, axis=0)


def node_features(place):
    ones = jnp.ones((3, place.shape[1]), F32)
    square = jnp.concatenate(
        split_three(place[0:1] ** 2 + place[1:2] ** 2 + place[2:3] ** 2), axis=0
    )
    tiles = product_tiles(place, True)
    gap = [row_mix(tiles[0], [ones])] + [row_mix(tile, []) for tile in tiles[1:]]
    far = [row_mix(tiles[0], [ones]), row_mix(tiles[1], [square])]
    far += [row_mix(tile, []) for tile in tiles[2:]]
    return gap, far


def segment_features(centre, normal):
    ones = jnp.ones((3, centre.shape[1]), F32)
    lean = centre[0:1] * normal[0:1] + centre[1:2] * normal[1:2] + centre[2:3] * normal[2:3]
    lean = jnp.concatenate(split_three(-lean), axis=0)
    square = centre[0:1] ** 2 + centre[1:2] ** 2 + centre[2:3] ** 2
    square = jnp.concatenate(split_three(square), axis=0)
    tiles = product_tiles(normal, False)
    gap = [row_mix(tiles[0], [lean])] + [row_mix(tile, []) for tile in tiles[1:]]
    tiles = product_tiles(-2.0 * centre, False)
    far = [row_mix(tiles[0], [square]), row_mix(tiles[1], [ones])]
    far += [row_mix(tile, []) for tile in tiles[2:]]
    return gap, far


FEATURES = 12 * ROWS
SCALE = math.sqrt(math.log2(math.e) / REACH)


def feature_kernel(step, own_ref, mask_ref, node_ref):
    cands = mask_ref.shape[1]

    def features(index, carry):
        start = pl.multiple_of(index * SEG, SEG)
        gap, far = node_features(own_ref[0:3, pl.ds(start, SEG)] * SCALE)
        mask = mask_ref[step, :, pl.ds(start, SEG)].astype(F32)
        for k in range(cands):
            live = mask[k : k + 1]
            rows = jnp.concatenate([tile * live for tile in gap] + far, axis=0)
            rows = jnp.concatenate([rows, jnp.zeros((SEG - FEATURES, SEG), F32)], axis=0)
            node_ref[k, pl.ds(start, SEG), :] = rows.T.astype(BF16)
        return carry

    lax.fori_loop(0, own_ref.shape[1] // SEG, features, 0, unroll=2)


def contact_kernel(
    step, list_any, node_ref, slots_ref, force_ref, react_ref, seg_ref, push_ref, list_ref, sem
):
    fetch = pltpu.make_async_copy(list_any, list_ref, sem)
    fetch.start()
    buckets = node_ref.shape[1] // SEG
    cands = node_ref.shape[0]
    slots = react_ref.shape[0]
    react_ref[...] = jnp.zeros_like(react_ref)

    def segments(index, carry):
        tile = slots_ref[pl.ds(pl.multiple_of(index * ROWS, ROWS), ROWS), :]
        gap, far = segment_features(tile[0:3] * SCALE, tile[3:6])
        blank = jnp.zeros((6 * ROWS, SEG), F32)
        left = jnp.concatenate(gap + [blank], axis=0)
        right = jnp.concatenate([blank] + far, axis=0)
        rows = jnp.concatenate([left, right], axis=1)
        seg_ref[index] = rows.astype(BF16)
        push = split_rows(tile[3:6])
        push = jnp.concatenate([push, push], axis=1)
        push_ref[index] = jnp.concatenate([push, jnp.zeros_like(push)], axis=0).astype(BF16)
        return carry

    lax.fori_loop(0, slots, segments, 0, unroll=4)
    fetch.wait()

    def bucket(index, carry):
        start = pl.multiple_of(index * SEG, SEG)
        total = jnp.zeros((2 * ROWS, SEG), F32)
        for k in range(cands):
            slot = list_ref[step, k, index]
            pair = jnp.dot(
                node_ref[k, pl.ds(start, SEG), :][:, :FEATURES],
                seg_ref[slot],
                preferred_element_type=F32,
            )
            gap, far = pair[:, :SEG], pair[:, SEG:]
            weight = jnp.minimum(gap, 0.0) * jnp.exp2(gap * gap - far)
            react_ref[pl.ds(slot, 1), :] += jnp.sum(weight, axis=0, keepdims=True)
            high = weight.astype(BF16)
            low = (weight - high.astype(F32)).astype(BF16)
            total = total + lax.dot_general(
                push_ref[slot],
                jnp.concatenate([high, low], axis=1),
                (((1,), (1,)), ((), ())),
                preferred_element_type=F32,
            )
        force = (total[0:3] + total[3:6]) * (-PENALTY / SCALE)
        force_ref[:, pl.ds(start, SEG)] = row_mix(force, [])
        return carry

    lax.fori_loop(0, buckets, bucket, 0, unroll=4)
    react_ref[...] = react_ref[...] * (-PENALTY / SCALE)


def internal_kernel(rows_ref, conn_ref, acc_ref):
    scatter_tiles(rows_ref, conn_ref, acc_ref)


def pick_kernel(picks_ref, conn_ref, tiles_ref):
    for step in range(tiles_ref.shape[0]):

        def copy(slot, carry):
            for half in range(2):
                row = conn_ref[pl.ds(picks_ref[step, slot] * 2 + half, 1), :]
                tiles_ref[step, pl.ds(slot * 2 + half, 1), :] = row
            return carry

        lax.fori_loop(0, tiles_ref.shape[1] // 2, copy, 0, unroll=8)


def collect_kernel(step, picks_ref, back_ref, seg_ref):
    seg_ref[...] = jnp.zeros_like(seg_ref)

    def collect(slot, carry):
        seg_ref[pl.ds(picks_ref[step, slot], 1), :] += back_ref[pl.ds(slot, 1), :]
        return carry

    lax.fori_loop(0, back_ref.shape[0], collect, 0)


def react_tiles(step, first, last, blocks_ref, back_ref, tiles_ref):
    def tile(index, total):
        react = back_ref[pl.ds(index, 1), :]
        normal = blocks_ref[pl.ds(pl.multiple_of(index * ROWS, ROWS), ROWS), :][3:6]
        rows = split_rows(-0.25 * react * normal)
        values = jnp.concatenate([rows, rows], axis=1)
        for half in range(2):
            ids = tiles_ref[step, pl.ds(index * 2 + half, 1), :]
            high_ids = ids >> 8
            spread = jnp.concatenate(
                [jnp.where(high_ids == part, values, 0.0) for part in range(first, last)], axis=0
            ).astype(BF16)
            total = total + lax.dot_general(
                spread,
                one_hot_low(ids & (LOW - 1)),
                (((1,), (1,)), ((), ())),
                preferred_element_type=F32,
            )
        return total

    start = jnp.zeros(((last - first) * ROWS, LOW), F32)
    return lax.fori_loop(0, back_ref.shape[0], tile, start, unroll=8)


def unstack(total):
    count = total.shape[0] // ROWS
    full = jnp.concatenate(
        [total[part * ROWS : (part + 1) * ROWS] for part in range(count)], axis=1
    )
    return row_mix(full[0:3] + full[3:6], [])


def react_ghost_kernel(step, blocks_ref, back_ref, tiles_ref, acc_ref, mesh_ref, sub_ref):
    last = acc_ref.shape[0] // ROWS
    first = last - (mesh_ref.shape[1] + sub_ref.shape[1]) // LOW
    total = react_tiles(step, first, last, blocks_ref, back_ref, tiles_ref)
    full = unstack(total + acc_ref[first * ROWS :, :])
    mesh_ref[...] = full[:, : mesh_ref.shape[1]]
    sub_ref[...] = full[:, mesh_ref.shape[1] :]


def react_own_kernel(step, blocks_ref, back_ref, tiles_ref, acc_ref, own_ref):
    last = own_ref.shape[1] // LOW
    total = react_tiles(step, 0, last, blocks_ref, back_ref, tiles_ref)
    own_ref[...] = unstack(total + acc_ref[: last * ROWS, :])


def scatter_tiles(rows_ref, conn_ref, acc_ref):
    count = acc_ref.shape[0] // ROWS
    acc_ref[...] = jnp.zeros_like(acc_ref)

    def tile(index, carry):
        ids = conn_ref[pl.ds(index, 1), :]
        start = pl.multiple_of(index * (LOW // SEG) * ROWS, ROWS * (LOW // SEG))
        parts = [rows_ref[pl.ds(start + half * ROWS, ROWS), :] for half in range(LOW // SEG)]
        values = jnp.concatenate(parts, axis=1)
        high_ids = ids >> 8
        spread = jnp.concatenate(
            [jnp.where(high_ids == part, values, 0.0) for part in range(count)], axis=0
        ).astype(BF16)
        acc_ref[...] += lax.dot_general(
            spread,
            one_hot_low(ids & (LOW - 1)),
            (((1,), (1,)), ((), ())),
            preferred_element_type=F32,
        )
        return carry

    lax.fori_loop(0, conn_ref.shape[0], tile, 0, unroll=UNROLL)


def add_back(back, ids_ref, count):
    total = jnp.zeros((count * ROWS, LOW), F32)
    high, low = split_two(back[0:3])
    pad = jnp.zeros((ROWS - 6, back.shape[1]), F32)
    rows = jnp.concatenate([high, low, pad], axis=0)
    for index in range(ids_ref.shape[0]):
        ids = ids_ref[index : index + 1, :]
        values = rows[:, index * LOW : (index + 1) * LOW]
        spread = jnp.concatenate(
            [jnp.where((ids >> 8) == part, values, 0.0) for part in range(count)], axis=0
        ).astype(BF16)
        total = total + lax.dot_general(
            spread,
            one_hot_low(ids & (LOW - 1)),
            (((1,), (1,)), ((), ())),
            preferred_element_type=F32,
        )
    return total


def pack_ghosts(own, ids_ref, out_ref):
    count = own.shape[1] // LOW
    tables = [stack_columns(part).astype(BF16) for part in split_three(own)]
    for index in range(ids_ref.shape[0]):
        ids = ids_ref[index : index + 1, :]
        hot = one_hot_low(ids & (LOW - 1))
        product = sum(jnp.dot(table, hot, preferred_element_type=F32) for table in tables)
        out_ref[:, index * LOW : (index + 1) * LOW] = pick_high(product, ids >> 8, count)


def pack_kernel(own_ref, mesh_ids_ref, sub_ids_ref, to_mesh_ref, to_sub_ref):
    own = own_ref[...]
    pack_ghosts(own, mesh_ids_ref, to_mesh_ref)
    pack_ghosts(own, sub_ids_ref, to_sub_ref)


def update_kernel(
    own_ref, force_ref, slave_ref, back_mesh_ref, back_sub_ref, mass_ref, mesh_ids_ref,
    sub_ids_ref, new_ref, to_mesh_ref, to_sub_ref,
):
    count = own_ref.shape[1] // LOW
    extra = add_back(back_mesh_ref[...], mesh_ids_ref, count) + add_back(
        back_sub_ref[...], sub_ids_ref, count
    )
    full = jnp.concatenate(
        [extra[part * ROWS : (part + 1) * ROWS] for part in range(count)], axis=1
    )
    force = force_ref[0:3, :] + slave_ref[0:3, :] + (full[0:3] + full[3:6])
    speed = own_ref[3:6, :] + TIME_STEP * force / mass_ref[...]
    place = own_ref[0:3, :] + TIME_STEP * speed
    own = jnp.concatenate([place, speed, jnp.zeros((ROWS - 6, place.shape[1]), F32)], axis=0)
    new_ref[...] = own
    if to_mesh_ref is not None:
        pack_ghosts(own, mesh_ids_ref, to_mesh_ref)
        pack_ghosts(own, sub_ids_ref, to_sub_ref)


def last_kernel(*refs):
    update_kernel(*refs, None, None)


VM = pl.BlockSpec(memory_space=pltpu.VMEM)
SM = pl.BlockSpec(memory_space=pltpu.SMEM)
ANY = pl.BlockSpec(memory_space=pl.ANY)


def call(kernel, outs, ins, scratch=(), flops=0):
    shapes = tuple(
        jax.ShapeDtypeStruct(shape, F32) if isinstance(shape, tuple) else shape for shape in outs
    )
    return pl.pallas_call(
        kernel,
        out_shape=shapes,
        in_specs=list(ins),
        out_specs=tuple(VM for _ in outs),
        scratch_shapes=[
            pltpu.VMEM(shape, F32) if isinstance(shape, tuple) else shape for shape in scratch
        ],
        compiler_params=pltpu.CompilerParams(vmem_limit_bytes=20 << 20),
        cost_estimate=pl.CostEstimate(flops=flops, bytes_accessed=1 << 20, transcendentals=0),
    )


def per_device(
    coords,
    veloc,
    node_mass,
    stress,
    connect,
    send_mesh,
    send_sub,
    send_pick,
    bucket_list,
    pair_mask,
):
    nodes = coords.shape[1]
    elems = stress.shape[1]
    ghost_mesh = send_mesh.shape[0]
    ghost_sub = send_sub.shape[0]
    width = nodes + ghost_mesh + ghost_sub
    peers = lax.axis_size("mesh")
    slots = send_pick.shape[1]
    per_peer = slots // peers
    blocks = elems // SEG
    conn = connect.reshape(4, blocks, SEG).transpose(1, 0, 2).reshape(4 * elems // LOW, LOW)
    mesh_ids = send_mesh.reshape(ghost_mesh // LOW, LOW)
    sub_ids = send_sub.reshape(ghost_sub // LOW, LOW)
    mass = node_mass.reshape(1, nodes)
    stress_now = stress.reshape(3, blocks, SEG)
    own = jnp.concatenate([coords, veloc, jnp.zeros((ROWS - 6, nodes), F32)], axis=0)

    chunks = nodes // SEG
    ghost_chunks = (ghost_mesh + ghost_sub) // SEG
    cands = bucket_list.shape[1]

    pack = call(pack_kernel, [(ROWS, ghost_mesh), (ROWS, ghost_sub)], [VM] * 3)
    own_rows_of = call(
        own_rows_kernel, [(2 * blocks * ROWS, SEG)], [VM] * 2, [(chunks, ROWS, SEG)], flops=1 << 31
    )
    geom = lambda step: call(
        functools.partial(geometry_kernel, step, nodes),
        [(12, blocks, SEG), (blocks * ROWS, SEG)] + [(slots * ROWS, SEG)] * 2,
        [ANY] + [VM] * 4,
        [
            (2 * blocks * ROWS, SEG),
            (ghost_chunks, ROWS, SEG),
            pltpu.SMEM(send_pick.shape, jnp.int32),
            pltpu.SemaphoreType.DMA,
        ],
        flops=1 << 30,
    )
    forces = call(
        force_kernel,
        [(4 * blocks * ROWS, SEG), (3, blocks, SEG)],
        [VM] * 6,
        [(4 * blocks * ROWS, SEG)],
        flops=1 << 31,
    )
    features = lambda step: call(
        functools.partial(feature_kernel, step),
        [jax.ShapeDtypeStruct((cands, nodes, SEG), BF16)],
        [VM] * 2,
        flops=1 << 30,
    )
    contact = lambda step: call(
        functools.partial(contact_kernel, step),
        [(ROWS, nodes), (slots, SEG)],
        [ANY] + [VM] * 2,
        [
            pltpu.VMEM((slots, FEATURES, 2 * SEG), BF16),
            pltpu.VMEM((slots, 2 * ROWS, 2 * SEG), BF16),
            pltpu.SMEM(bucket_list.shape, jnp.int32),
            pltpu.SemaphoreType.DMA,
        ],
        flops=1 << 31,
    )
    internal_of = call(internal_kernel, [(width // LOW * ROWS, LOW)], [VM] * 2, flops=1 << 31)
    react_ghost = lambda step: call(
        functools.partial(react_ghost_kernel, step),
        [(ROWS, ghost_mesh), (ROWS, ghost_sub)],
        [VM] * 4,
        flops=1 << 29,
    )
    react_own = lambda step: call(
        functools.partial(react_own_kernel, step), [(ROWS, nodes)], [VM] * 4, flops=1 << 30
    )
    update = call(update_kernel, [(ROWS, nodes), (ROWS, ghost_mesh), (ROWS, ghost_sub)], [VM] * 8)
    finish = call(last_kernel, [(ROWS, nodes)], [VM] * 8)

    by_slot = slots <= blocks
    pick_tiles = call(
        pick_kernel,
        [jax.ShapeDtypeStruct((STEPS, slots * 2, LOW), jnp.int32)],
        [SM, VM],
        flops=1 << 20,
    )
    collect = lambda step: call(functools.partial(collect_kernel, step), [(blocks, SEG)], [SM, VM])

    to_mesh, to_sub = pack(own, mesh_ids, sub_ids)
    tiles = pick_tiles(send_pick, conn)[0] if by_slot else conn[None]
    for step in range(STEPS):
        from_mesh = shifted(to_mesh, "mesh", 1)
        from_sub = shifted(to_sub, "sub", 1)
        (own_rows,) = own_rows_of(own, conn)
        (node,) = features(step)(own, pair_mask)
        corner, geo, outgoing, kept = geom(step)(
            send_pick, from_mesh, from_sub, conn, own_rows
        )
        incoming = lax.all_to_all(
            outgoing.reshape(peers, per_peer * ROWS, SEG),
            "mesh", split_axis=0, concat_axis=0, tiled=True,
        ).reshape(slots * ROWS, SEG)
        pushes, stress_now = forces(own, from_mesh, from_sub, conn, corner, stress_now)
        slave, react = contact(step)(bucket_list, node, incoming)
        returned = lax.all_to_all(
            react.reshape(peers, per_peer, SEG),
            "mesh", split_axis=0, concat_axis=0, tiled=True,
        ).reshape(slots, SEG)
        (acc,) = internal_of(pushes, conn)
        if by_slot:
            rows = (kept, returned, tiles, acc)
        else:
            rows = (geo, collect(step)(send_pick, returned)[0], tiles, acc)
        at = step if by_slot else 0
        back_mesh, back_sub = react_ghost(at)(*rows)
        (force,) = react_own(at)(*rows)
        back_mesh = shifted(back_mesh, "mesh", -1)
        back_sub = shifted(back_sub, "sub", -1)
        args = (own, force, slave, back_mesh, back_sub, mass, mesh_ids, sub_ids)
        if step < STEPS - 1:
            own, to_mesh, to_sub = update(*args)
        else:
            (own,) = finish(*args)
    return own[3:6], stress_now.reshape(3, elems)


def solution(mesh):
    return jax.shard_map(
        per_device,
        mesh=mesh,
        in_specs=(
            P(None, ("mesh", "sub")),
            P(None, ("mesh", "sub")),
            P(("mesh", "sub")),
            P(None, ("mesh", "sub")),
            P(None, ("mesh", "sub")),
            P(("mesh", "sub")),
            P(("mesh", "sub")),
            P(None, ("mesh", "sub")),
            P(None, None, ("mesh", "sub")),
            P(None, None, ("mesh", "sub")),
        ),
        out_specs=(P(None, ("mesh", "sub")), P(None, ("mesh", "sub"))),
        check_vma=False,
    )
```

```python
import functools
import math

import jax
import jax.numpy as jnp
from jax import lax
from jax.experimental import pallas as pl
from jax.experimental.pallas import tpu as pltpu
from jax.sharding import PartitionSpec as P


SEG = 128
STEPS = 4
LOW = 256
ROWS = 8
SENT = 6
UNROLL = 8

TIME_STEP = 0.2
YOUNG = 1.0
POISSON = 0.3
HOURGLASS = 0.01
PENALTY = 0.2
REACH = 4.0
HOUR_SIGNS = (1.0, -1.0, 1.0, -1.0)

F32 = jnp.float32
BF16 = jnp.bfloat16


def shifted(value, axis, steps):
    count = lax.axis_size(axis)
    pairs = [(source, (source + steps) % count) for source in range(count)]
    return lax.ppermute(value, axis, pairs)


def split_two(value):
    high = value.astype(BF16).astype(F32)
    return high, value - high


def split_three(value):
    high = value.astype(BF16).astype(F32)
    rest = value - high
    mid = rest.astype(BF16).astype(F32)
    return high, mid, rest - mid


def one_hot_low(low_ids, low=LOW):
    width = low_ids.shape[1]
    rows = lax.broadcasted_iota(jnp.int32, (low, width), 0)
    return jnp.where(rows == low_ids, 1.0, 0.0).astype(BF16)


def stack_columns(rows_eight):
    count = rows_eight.shape[1] // LOW
    return jnp.concatenate(
        [rows_eight[:, part * LOW : (part + 1) * LOW] for part in range(count)], axis=0
    )


def pick_high(product, high_ids, count):
    width = product.shape[1]
    total = jnp.zeros((ROWS, width), F32)
    for part in range(count):
        total = jnp.where(high_ids == part, product[part * ROWS : (part + 1) * ROWS], total)
    return total


def split_rows(three):
    high, low = split_two(three)
    pad = jnp.zeros((ROWS - 6, three.shape[1]), F32)
    return jnp.concatenate([high, low, pad], axis=0)


def corner_ids(conn_ref, block):
    return conn_ref[:, pl.ds(pl.multiple_of(block * SEG, SEG), SEG)]


def pair_row(ids, half):
    return jnp.concatenate([ids[2 * half : 2 * half + 1], ids[2 * half + 1 : 2 * half + 2]], axis=1)


def pair_lanes(ids, half):
    rows = [jnp.broadcast_to(ids[2 * half + i : 2 * half + i + 1], (4, SEG)) for i in range(2)]
    return jnp.concatenate(rows, axis=0)


def gather_tiles(table, conn_ref, out_ref):
    count = table.shape[0] // ROWS

    def tile(block, carry):
        corners = corner_ids(conn_ref, block)
        for half in range(2):
            ids = pair_row(corners, half)
            product = jnp.dot(table, one_hot_low(ids & (LOW - 1)), preferred_element_type=F32)
            total = pick_high(product, ids >> 8, count)
            for i in range(2):
                start = pl.multiple_of((block * 4 + half * 2 + i) * ROWS, ROWS)
                out_ref[pl.ds(start, ROWS), :] = total[:, i * SEG : (i + 1) * SEG]
        return carry

    lax.fori_loop(0, conn_ref.shape[1] // SEG, tile, 0, unroll=UNROLL // 2)


def cross(left, right):
    return (
        left[1] * right[2] - left[2] * right[1],
        left[2] * right[0] - left[0] * right[2],
        left[0] * right[1] - left[1] * right[0],
    )


def sub3(left, right):
    return tuple(a - b for a, b in zip(left, right))


def dot3(left, right):
    return left[0] * right[0] + left[1] * right[1] + left[2] * right[2]


def geometry(corner):
    raw = cross(sub3(corner[2], corner[0]), sub3(corner[3], corner[1]))
    twice_area = jnp.maximum(jnp.sqrt(dot3(raw, raw)), 1.0)
    inverse = 1.0 / twice_area
    normal = tuple(part * inverse for part in raw)
    centre = tuple(
        0.25 * (corner[0][c] + corner[1][c] + corner[2][c] + corner[3][c]) for c in range(3)
    )
    return centre, normal, twice_area, inverse


def corner_rows(ref, group, component):
    return [
        ref[pl.ds((group * 32 + corner) * ROWS + component, 8, stride=4 * ROWS), :]
        for corner in range(4)
    ]


def tree_pick(values, bits):
    level = 0
    while len(values) > 1:
        values = [
            jnp.where(bits[level], values[i + 1], values[i]) if i + 1 < len(values) else values[i]
            for i in range(0, len(values), 2)
        ]
        level += 1
    return values[0]


def fill_chunks(three, chunk_ref, first):
    four = jnp.concatenate([three, jnp.zeros((1, three.shape[1]), F32)], axis=0)
    twice = jnp.concatenate([four, four], axis=0)
    for part in range(three.shape[1] // SEG):
        chunk_ref[first + part] = twice[:, part * SEG : (part + 1) * SEG]


def lane_pick(chunk_ref, ids, high_ids):
    count = chunk_ref.shape[0]
    low_ids = ids & (SEG - 1)
    bits = [((high_ids >> bit) & 1) == 1 for bit in range((count - 1).bit_length())]
    values = [
        jnp.take_along_axis(chunk_ref[part], low_ids, axis=1, mode="promise_in_bounds")
        for part in range(count)
    ]
    return tree_pick(values, bits)


def own_rows_kernel(own_ref, conn_ref, rows_ref, chunk_ref):
    fill_chunks(own_ref[0:3, :], chunk_ref, 0)

    def tile(block, carry):
        corners = corner_ids(conn_ref, block)
        for half in range(2):
            ids = pair_lanes(corners, half)
            start = pl.multiple_of((block * 2 + half) * ROWS, ROWS)
            rows_ref[pl.ds(start, ROWS), :] = lane_pick(chunk_ref, ids, ids >> 7)
        return carry

    lax.fori_loop(0, conn_ref.shape[1] // SEG, tile, 0, unroll=4)


def geometry_kernel(
    step, nodes, picks_any, mesh_ref, sub_ref, conn_ref, own_rows_ref, corner_ref, geo_ref,
    out_ref, kept_ref, rows_ref, chunk_ref, picks_ref, sem,
):
    fetch = pltpu.make_async_copy(picks_any, picks_ref, sem)
    fetch.start()
    blocks = geo_ref.shape[0] // ROWS
    first = mesh_ref.shape[1] // SEG
    fill_chunks(mesh_ref[0:3, :], chunk_ref, 0)
    fill_chunks(sub_ref[0:3, :], chunk_ref, first)

    def tile(block, carry):
        corners = corner_ids(conn_ref, block)
        for half in range(2):
            ids = pair_lanes(corners, half)
            start = pl.multiple_of((block * 2 + half) * ROWS, ROWS)
            far = lane_pick(chunk_ref, ids, (ids >> 7) - nodes // SEG)
            near = own_rows_ref[pl.ds(start, ROWS), :]
            rows_ref[pl.ds(start, ROWS), :] = jnp.where(ids >= nodes, far, near)
        return carry

    lax.fori_loop(0, conn_ref.shape[1] // SEG, tile, 0, unroll=16)
    for group in range(blocks // 8):
        corner = [
            tuple(rows_ref[pl.ds(group * 128 + i * 4 + c, 8, stride=16), :] for c in range(3))
            for i in range(4)
        ]
        for i in range(4):
            for c in range(3):
                corner_ref[i * 3 + c, group * 8 : (group + 1) * 8, :] = corner[i][c]
        centre, normal, _, _ = geometry(corner)
        for c in range(3):
            geo_ref[pl.ds(group * 8 * ROWS + c, 8, stride=ROWS), :] = centre[c]
            geo_ref[pl.ds(group * 8 * ROWS + 3 + c, 8, stride=ROWS), :] = normal[c]
        for c in range(6, ROWS):
            geo_ref[pl.ds(group * 8 * ROWS + c, 8, stride=ROWS), :] = jnp.zeros((8, SEG), F32)

    fetch.wait()
    peers, groups = out_ref.shape[:2]
    per_peer = picks_ref.shape[1] // peers
    for peer in range(peers):
        rows = []
        for slot in range(peer * per_peer, (peer + 1) * per_peer):
            start = pl.multiple_of(picks_ref[step, slot] * ROWS, ROWS)
            block = geo_ref[pl.ds(start, ROWS), :]
            rows.append(block[:SENT])
            if kept_ref is not None:
                kept_ref[slot * ROWS : (slot + 1) * ROWS, :] = block
        rows.append(jnp.zeros((groups * 4 - per_peer * SENT, SEG), F32))
        rows = jnp.concatenate([part for part in rows if part.shape[0]], axis=0)
        for group in range(groups):
            out_ref[peer, group] = rows[group * 4 : (group + 1) * 4]


def geometry_slots_kernel(step, nodes, *refs):
    ins, (corner_ref, kept_ref, out_ref), (geo_ref, *scratch) = refs[:5], refs[5:8], refs[8:]
    geometry_kernel(step, nodes, *ins, corner_ref, geo_ref, out_ref, kept_ref, *scratch)


def geometry_blocks_kernel(step, nodes, *refs):
    geometry_kernel(step, nodes, *refs[:8], None, *refs[8:])


def force_kernel(
    own_ref, mesh_ref, sub_ref, conn_ref, corner_ref, stress_ref, push_ref, new_ref, rows_ref
):
    blocks = corner_ref.shape[1]
    full = jnp.concatenate([own_ref[3:6, :], mesh_ref[3:6, :], sub_ref[3:6, :]], axis=1)
    gather_tiles(stack_columns(split_rows(full)).astype(BF16), conn_ref, rows_ref)
    stiff = YOUNG / (1.0 - POISSON * POISSON)
    for group in range(blocks // 8):
        here = slice(group * 8, (group + 1) * 8)
        speed_parts = []
        for component in range(3):
            high = corner_rows(rows_ref, group, component)
            low = corner_rows(rows_ref, group, component + 3)
            speed_parts.append([a + b for a, b in zip(high, low)])
        speed = [tuple(speed_parts[c][i] for c in range(3)) for i in range(4)]
        corner = [tuple(corner_ref[i * 3 + c, here, :] for c in range(3)) for i in range(4)]
        centre, normal, twice_area, inverse = geometry(corner)
        side = sub3(corner[1], corner[0])
        side_inverse = 1.0 / jnp.maximum(jnp.sqrt(dot3(side, side)), 1.0)
        axis_one = tuple(part * side_inverse for part in side)
        axis_two = cross(normal, axis_one)
        relative = [sub3(corner[i], centre) for i in range(4)]
        x = [dot3(relative[i], axis_one) for i in range(4)]
        y = [dot3(relative[i], axis_two) for i in range(4)]
        u = [dot3(speed[i], axis_one) for i in range(4)]
        v = [dot3(speed[i], axis_two) for i in range(4)]
        y13, y20 = (y[1] - y[3]) * inverse, (y[2] - y[0]) * inverse
        x31, x02 = (x[3] - x[1]) * inverse, (x[0] - x[2]) * inverse
        bx = [y13, y20, -y13, -y20]
        by = [x31, x02, -x31, -x02]
        u02, u13, v02, v13 = u[0] - u[2], u[1] - u[3], v[0] - v[2], v[1] - v[3]
        rate_xx = y13 * u02 + y20 * u13
        rate_yy = x31 * v02 + x02 * v13
        rate_xy = x31 * u02 + x02 * u13 + y13 * v02 + y20 * v13
        s0 = stress_ref[0, here, :] + TIME_STEP * (stiff * (rate_xx + POISSON * rate_yy))
        s1 = stress_ref[1, here, :] + TIME_STEP * (stiff * (POISSON * rate_xx + rate_yy))
        s2 = stress_ref[2, here, :] + TIME_STEP * (YOUNG / (2.0 * (1.0 + POISSON)) * rate_xy)
        new_ref[0, here, :] = s0
        new_ref[1, here, :] = s1
        new_ref[2, here, :] = s2
        half_area = 0.5 * twice_area
        hour_x = x[0] - x[1] + x[2] - x[3]
        hour_y = y[0] - y[1] + y[2] - y[3]
        shape = [HOUR_SIGNS[i] - hour_x * bx[i] - hour_y * by[i] for i in range(4)]
        rate = tuple(
            HOURGLASS * sum(shape[i] * speed[i][c] for i in range(4)) for c in range(3)
        )
        for i in range(4):
            force_x = half_area * (bx[i] * s0 + by[i] * s2)
            force_y = half_area * (by[i] * s1 + bx[i] * s2)
            start = (group * 32 + i) * ROWS
            for c in range(3):
                internal = force_x * axis_one[c] + force_y * axis_two[c] + shape[i] * rate[c]
                high, low = split_two(-internal)
                push_ref[pl.ds(start + c, 8, stride=4 * ROWS), :] = high
                push_ref[pl.ds(start + 3 + c, 8, stride=4 * ROWS), :] = low
            for c in range(6, ROWS):
                push_ref[pl.ds(start + c, 8, stride=4 * ROWS), :] = jnp.zeros((8, SEG), F32)


def product_tiles(value, turn):
    parts = split_three(value)
    order = (0, 0, 1, 0, 1, 2) if turn else (0, 1, 0, 2, 1, 0)
    return [parts[index] for index in order]


def row_mix(three, extras):
    width = three.shape[1]
    rows = [three] + extras
    pad = -sum(part.shape[0] for part in rows) % ROWS
    if pad:
        rows.append(jnp.zeros((pad, width), F32))
    return jnp.concatenate(rows, axis=0)


def node_features(place):
    ones = jnp.ones((3, place.shape[1]), F32)
    square = jnp.concatenate(
        split_three(place[0:1] ** 2 + place[1:2] ** 2 + place[2:3] ** 2), axis=0
    )
    tiles = product_tiles(place, True)
    return row_mix(tiles[0], tiles[1:] + [ones]), row_mix(tiles[0], tiles[1:] + [ones, square])


def segment_features(centre, normal):
    ones = jnp.ones((3, centre.shape[1]), F32)
    lean = centre[0:1] * normal[0:1] + centre[1:2] * normal[1:2] + centre[2:3] * normal[2:3]
    lean = jnp.concatenate(split_three(-lean), axis=0)
    square = centre[0:1] ** 2 + centre[1:2] ** 2 + centre[2:3] ** 2
    square = jnp.concatenate(split_three(square), axis=0)
    tiles = product_tiles(normal, False)
    gap = row_mix(tiles[0], tiles[1:] + [lean])
    tiles = product_tiles(-2.0 * centre, False)
    return gap, row_mix(tiles[0], tiles[1:] + [square, ones])


FEATURES = 6 * ROWS
SCALE = math.sqrt(math.log2(math.e) / REACH)


def feature_kernel(step, own_ref, mask_ref, node_ref):
    cands = mask_ref.shape[1]

    def features(index, carry):
        start = pl.multiple_of(index * SEG, SEG)
        gap, far = node_features(own_ref[0:3, pl.ds(start, SEG)] * SCALE)
        mask = mask_ref[step, :, pl.ds(start, SEG)].astype(F32)
        for k in range(cands):
            live = mask[k : k + 1]
            rows = jnp.concatenate([gap * live, far], axis=0)
            rows = jnp.concatenate([rows, jnp.zeros((SEG - FEATURES, SEG), F32)], axis=0)
            node_ref[k, pl.ds(start, SEG), :] = rows.T.astype(BF16)
        return carry

    lax.fori_loop(0, own_ref.shape[1] // SEG, features, 0, unroll=2)


def contact_kernel(
    step, list_any, node_ref, slots_ref, force_ref, react_ref, seg_ref, push_ref, list_ref, sem
):
    fetch = pltpu.make_async_copy(list_any, list_ref, sem)
    fetch.start()
    buckets = node_ref.shape[1] // SEG
    cands = node_ref.shape[0]
    slots = react_ref.shape[0]
    react_ref[...] = jnp.zeros_like(react_ref)

    peers, groups = slots_ref.shape[:2]
    per_peer = slots // peers
    for index in range(slots):
        if index % per_peer == 0:
            rows = [slots_ref[index // per_peer, group] for group in range(groups)]
            rows = jnp.concatenate(rows, axis=0)
        tile = rows[index % per_peer * SENT : (index % per_peer + 1) * SENT]
        gap, far = segment_features(tile[0:3] * SCALE, tile[3:6])
        blank = jnp.zeros((FEATURES // 2, SEG), F32)
        left = jnp.concatenate([gap, blank], axis=0)
        right = jnp.concatenate([blank, far], axis=0)
        seg_ref[index] = jnp.concatenate([left, right], axis=1).astype(BF16)
        push = split_rows(tile[3:6])
        push = jnp.concatenate([push, push], axis=1)
        push_ref[index] = jnp.concatenate([push, jnp.zeros_like(push)], axis=0).astype(BF16)
    fetch.wait()

    def bucket(index, carry):
        start = pl.multiple_of(index * SEG, SEG)
        chosen = [list_ref[step, k, index] for k in range(cands)]
        pairs = [
            jnp.dot(
                node_ref[k, pl.ds(start, SEG), :][:, :FEATURES],
                seg_ref[chosen[k]],
                preferred_element_type=F32,
            )
            for k in range(cands)
        ]
        parts = []
        for k in range(cands):
            gap, far = pairs[k][:, :SEG], pairs[k][:, SEG:]
            weight = jnp.minimum(gap, 0.0) * jnp.exp2(gap * gap - far)
            react_ref[pl.ds(chosen[k], 1), :] += jnp.sum(weight, axis=0, keepdims=True)
            high = weight.astype(BF16)
            low = (weight - high.astype(F32)).astype(BF16)
            parts.append(jnp.concatenate([high, low], axis=1))
        total = dot_rows(
            jnp.concatenate([push_ref[slot] for slot in chosen], axis=1),
            jnp.concatenate(parts, axis=1),
        )
        force = (total[0:3] + total[3:6]) * (-PENALTY / SCALE)
        force_ref[:, pl.ds(start, SEG)] = row_mix(force, [])
        return carry

    lax.fori_loop(0, buckets, bucket, 0, unroll=16)
    react_ref[...] = react_ref[...] * (-PENALTY / SCALE)


def internal_kernel(rows_ref, conn_ref, acc_ref):
    scatter_tiles(rows_ref, conn_ref, acc_ref)


def pick_kernel(picks_ref, conn_ref, tiles_ref):
    for step in range(tiles_ref.shape[0]):

        def copy(slot, carry):
            tiles_ref[step, slot] = corner_ids(conn_ref, picks_ref[step, slot])
            return carry

        lax.fori_loop(0, tiles_ref.shape[1], copy, 0, unroll=8)


def collect_kernel(step, picks_ref, back_ref, seg_ref):
    seg_ref[...] = jnp.zeros_like(seg_ref)

    def collect(slot, carry):
        seg_ref[pl.ds(picks_ref[step, slot], 1), :] += back_ref[pl.ds(slot, 1), :]
        return carry

    lax.fori_loop(0, back_ref.shape[0], collect, 0)


def react_tiles(step, first, last, low, unroll, blocks_ref, back_ref, tiles_ref):
    def tile(index, total):
        react = back_ref[pl.ds(index, 1), :]
        normal = blocks_ref[pl.ds(pl.multiple_of(index * ROWS, ROWS), ROWS), :][3:6]
        rows = split_rows(-0.25 * react * normal)
        values = jnp.concatenate([rows, rows], axis=1)
        corners = tiles_ref[step, index]
        for half in range(2):
            ids = pair_row(corners, half)
            spread = spread_rows(values, ids, first, last, low)
            total = total + dot_rows(spread, one_hot_low(ids & (low - 1), low))
        return total

    start = jnp.zeros(((last - first) * ROWS, low), F32)
    return lax.fori_loop(0, back_ref.shape[0], tile, start, unroll=unroll)


def unstack(total):
    count = total.shape[0] // ROWS
    full = jnp.concatenate(
        [total[part * ROWS : (part + 1) * ROWS] for part in range(count)], axis=1
    )
    return row_mix(full[0:3] + full[3:6], [])


def react_ghost_kernel(step, blocks_ref, back_ref, tiles_ref, acc_ref, mesh_ref, sub_ref):
    count = acc_ref.shape[0] // ROWS
    ghosts = mesh_ref.shape[1] + sub_ref.shape[1]
    first, last = count * LOW // SEG - ghosts // SEG, count * LOW // SEG
    total = react_tiles(step, first, last, SEG, 16, blocks_ref, back_ref, tiles_ref)
    full = unstack(total) + unstack(acc_ref[(count - ghosts // LOW) * ROWS :, :])
    mesh_ref[...] = full[:, : mesh_ref.shape[1]]
    sub_ref[...] = full[:, mesh_ref.shape[1] :]


def react_own_kernel(step, blocks_ref, back_ref, tiles_ref, acc_ref, own_ref):
    last = own_ref.shape[1] // LOW
    total = react_tiles(step, 0, last, LOW, 8, blocks_ref, back_ref, tiles_ref)
    own_ref[...] = unstack(total + acc_ref[: last * ROWS, :])


def spread_rows(values, ids, first, last, low=LOW):
    high_ids = ids >> (low.bit_length() - 1)
    parts = [jnp.where(high_ids == part, values, 0.0) for part in range(first, last)]
    return jnp.concatenate(parts, axis=0).astype(BF16)


def dot_rows(left, right):
    return lax.dot_general(left, right, (((1,), (1,)), ((), ())), preferred_element_type=F32)


def scatter_tiles(rows_ref, conn_ref, acc_ref):
    count = acc_ref.shape[0] // ROWS
    acc_ref[...] = jnp.zeros_like(acc_ref)

    def tile(block, carry):
        corners = corner_ids(conn_ref, block)
        for half in range(2):
            ids = pair_row(corners, half)
            start = pl.multiple_of((block * 2 + half) * 2 * ROWS, 2 * ROWS)
            parts = [rows_ref[pl.ds(start + i * ROWS, ROWS), :] for i in range(2)]
            spread = spread_rows(jnp.concatenate(parts, axis=1), ids, 0, count)
            acc_ref[...] += dot_rows(spread, one_hot_low(ids & (LOW - 1)))
        return carry

    lax.fori_loop(0, conn_ref.shape[1] // SEG, tile, 0, unroll=UNROLL // 2)


def add_back(back, ids_ref, count):
    rows = split_rows(back[0:3])
    total = jnp.zeros((count * ROWS, LOW), F32)
    for index in range(back.shape[1] // LOW):
        here = slice(index * LOW, (index + 1) * LOW)
        ids = ids_ref[:, here]
        spread = spread_rows(rows[:, here], ids, 0, count)
        total = total + dot_rows(spread, one_hot_low(ids & (LOW - 1)))
    return total


def pack_ghosts(table, ids_ref, out_ref):
    count = table.shape[0] // (3 * ROWS)
    size = count * ROWS
    for index in range(out_ref.shape[1] // LOW):
        here = slice(index * LOW, (index + 1) * LOW)
        ids = ids_ref[:, here]
        product = jnp.dot(table, one_hot_low(ids & (LOW - 1)), preferred_element_type=F32)
        product = product[:size] + product[size : 2 * size] + product[2 * size :]
        out_ref[:, here] = pick_high(product, ids >> 8, count)


def pack_both(own, mesh_ids_ref, sub_ids_ref, to_mesh_ref, to_sub_ref):
    parts = [stack_columns(part) for part in split_three(own)]
    table = jnp.concatenate(parts, axis=0).astype(BF16)
    pack_ghosts(table, mesh_ids_ref, to_mesh_ref)
    pack_ghosts(table, sub_ids_ref, to_sub_ref)


def pack_kernel(
    coords_any, veloc_any, mesh_any, sub_any, own_ref, to_mesh_ref, to_sub_ref, coords_ref,
    veloc_ref, mesh_ids_ref, sub_ids_ref, sems,
):
    sources = (coords_any, veloc_any, mesh_any, sub_any)
    targets = (coords_ref, veloc_ref, mesh_ids_ref, sub_ids_ref)
    copies = [
        pltpu.make_async_copy(source, target, sems.at[index])
        for index, (source, target) in enumerate(zip(sources, targets))
    ]
    for copy in copies:
        copy.start()
    for copy in copies:
        copy.wait()
    pad = jnp.zeros((ROWS - 6, coords_ref.shape[1]), F32)
    own = jnp.concatenate([coords_ref[...], veloc_ref[...], pad], axis=0)
    own_ref[...] = own
    pack_both(own, mesh_ids_ref, sub_ids_ref, to_mesh_ref, to_sub_ref)


def new_state(
    own_ref, force_ref, slave_ref, back_mesh_ref, back_sub_ref, mass_ref, mesh_ids_ref,
    sub_ids_ref,
):
    count = own_ref.shape[1] // LOW
    extra = add_back(back_mesh_ref[...], mesh_ids_ref, count) + add_back(
        back_sub_ref[...], sub_ids_ref, count
    )
    full = unstack(extra)
    force = force_ref[0:3, :] + slave_ref[0:3, :] + full[0:3]
    return own_ref[3:6, :] + TIME_STEP * force / mass_ref[...]


def update_kernel(*refs):
    own_ref, mesh_ids_ref, sub_ids_ref = refs[0], refs[6], refs[7]
    new_ref, to_mesh_ref, to_sub_ref = refs[8:]
    speed = new_state(*refs[:8])
    place = own_ref[0:3, :] + TIME_STEP * speed
    own = jnp.concatenate([place, speed, jnp.zeros((ROWS - 6, place.shape[1]), F32)], axis=0)
    new_ref[...] = own
    pack_both(own, mesh_ids_ref, sub_ids_ref, to_mesh_ref, to_sub_ref)


def last_kernel(*refs):
    refs[8][...] = new_state(*refs[:8])


VM = pl.BlockSpec(memory_space=pltpu.VMEM)
SM = pl.BlockSpec(memory_space=pltpu.SMEM)
ANY = pl.BlockSpec(memory_space=pl.ANY)
HBM = pl.BlockSpec(memory_space=pltpu.HBM)


def call(kernel, outs, ins, scratch=(), flops=0):
    shapes = tuple(
        jax.ShapeDtypeStruct(shape, F32) if isinstance(shape, tuple) else shape for shape in outs
    )
    return pl.pallas_call(
        kernel,
        out_shape=shapes,
        in_specs=list(ins),
        out_specs=tuple(VM for _ in outs),
        scratch_shapes=[
            pltpu.VMEM(shape, F32) if isinstance(shape, tuple) else shape for shape in scratch
        ],
        compiler_params=pltpu.CompilerParams(vmem_limit_bytes=8 << 20),
        cost_estimate=pl.CostEstimate(flops=flops, bytes_accessed=1 << 20, transcendentals=0),
    )


def per_device(
    coords,
    veloc,
    node_mass,
    stress,
    connect,
    send_mesh,
    send_sub,
    send_pick,
    bucket_list,
    pair_mask,
):
    nodes = coords.shape[1]
    elems = stress.shape[1]
    ghost_mesh = send_mesh.shape[0]
    ghost_sub = send_sub.shape[0]
    width = nodes + ghost_mesh + ghost_sub
    peers = lax.axis_size("mesh")
    slots = send_pick.shape[1]
    per_peer = slots // peers
    blocks = elems // SEG
    mesh_ids = send_mesh.reshape(1, ghost_mesh)
    sub_ids = send_sub.reshape(1, ghost_sub)
    mass = node_mass.reshape(1, nodes)
    stress_now = stress.reshape(3, blocks, SEG)
    conn = connect

    chunks = nodes // SEG
    ghost_chunks = (ghost_mesh + ghost_sub) // SEG
    cands = bucket_list.shape[1]

    pack = call(
        pack_kernel,
        [
            (ROWS, nodes),
            (ROWS, ghost_mesh),
            (ROWS, ghost_sub),
        ],
        [HBM] * 4,
        [
            (3, nodes),
            (3, nodes),
            pltpu.VMEM((1, ghost_mesh), jnp.int32),
            pltpu.VMEM((1, ghost_sub), jnp.int32),
            pltpu.SemaphoreType.DMA((4,)),
        ],
    )
    own_rows_of = call(
        own_rows_kernel, [(2 * blocks * ROWS, SEG)], [VM] * 2, [(chunks, ROWS, SEG)], flops=1 << 31
    )
    by_slot = slots <= blocks
    geom = lambda step: call(
        functools.partial(
            geometry_slots_kernel if by_slot else geometry_blocks_kernel, step, nodes
        ),
        [
            (12, blocks, SEG),
            (slots * ROWS if by_slot else blocks * ROWS, SEG),
            (peers, pl.cdiv(per_peer * SENT, 4), 4, SEG),
        ],
        [ANY] + [VM] * 4,
        ([(blocks * ROWS, SEG)] if by_slot else [])
        + [
            (2 * blocks * ROWS, SEG),
            (ghost_chunks, ROWS, SEG),
            pltpu.SMEM(send_pick.shape, jnp.int32),
            pltpu.SemaphoreType.DMA,
        ],
        flops=1 << 30,
    )
    forces = call(
        force_kernel,
        [(4 * blocks * ROWS, SEG), (3, blocks, SEG)],
        [VM] * 6,
        [(4 * blocks * ROWS, SEG)],
        flops=1 << 31,
    )
    features = lambda step: call(
        functools.partial(feature_kernel, step),
        [jax.ShapeDtypeStruct((cands, nodes, SEG), BF16)],
        [VM] * 2,
        flops=1 << 30,
    )
    contact = lambda step: call(
        functools.partial(contact_kernel, step),
        [(ROWS, nodes), (slots, SEG)],
        [ANY] + [VM] * 2,
        [
            pltpu.VMEM((slots, FEATURES, 2 * SEG), BF16),
            pltpu.VMEM((slots, 2 * ROWS, 2 * SEG), BF16),
            pltpu.SMEM(bucket_list.shape, jnp.int32),
            pltpu.SemaphoreType.DMA,
        ],
        flops=1 << 31,
    )
    internal_of = call(internal_kernel, [(width // LOW * ROWS, LOW)], [VM] * 2, flops=1 << 31)
    react_ghost = lambda step: call(
        functools.partial(react_ghost_kernel, step),
        [(ROWS, ghost_mesh), (ROWS, ghost_sub)],
        [VM] * 4,
        flops=1 << 29,
    )
    react_own = lambda step: call(
        functools.partial(react_own_kernel, step), [(ROWS, nodes)], [VM] * 4, flops=1 << 30
    )
    update = call(update_kernel, [(ROWS, nodes), (ROWS, ghost_mesh), (ROWS, ghost_sub)], [VM] * 8)
    finish = call(last_kernel, [(3, nodes)], [VM] * 8)

    pick_tiles = call(
        pick_kernel,
        [jax.ShapeDtypeStruct((STEPS, slots, 4, SEG), jnp.int32)],
        [SM, VM],
        flops=1 << 20,
    )
    collect = lambda step: call(functools.partial(collect_kernel, step), [(blocks, SEG)], [SM, VM])

    own, to_mesh, to_sub = pack(
        *[pltpu.with_memory_space_constraint(x, pltpu.HBM) for x in (coords, veloc, mesh_ids, sub_ids)]
    )
    if by_slot:
        (tiles,) = pick_tiles(send_pick, conn)
    else:
        tiles = conn.reshape(4, blocks, SEG).transpose(1, 0, 2)[None]
    for step in range(STEPS):
        from_mesh = shifted(to_mesh, "mesh", 1)
        from_sub = shifted(to_sub, "sub", 1)
        (own_rows,) = own_rows_of(own, conn)
        (node,) = features(step)(own, pair_mask)
        corner, kept, outgoing = geom(step)(
            send_pick, from_mesh, from_sub, conn, own_rows
        )
        incoming = lax.all_to_all(
            outgoing, "mesh", split_axis=0, concat_axis=0, tiled=True
        )
        pushes, stress_now = forces(own, from_mesh, from_sub, conn, corner, stress_now)
        slave, react = contact(step)(bucket_list, node, incoming)
        returned = lax.all_to_all(
            react.reshape(peers, per_peer, SEG),
            "mesh", split_axis=0, concat_axis=0, tiled=True,
        ).reshape(slots, SEG)
        (acc,) = internal_of(pushes, conn)
        at = step if by_slot else 0
        if by_slot:
            rows = (kept, returned, tiles, acc)
        else:
            rows = (kept, collect(step)(send_pick, returned)[0], tiles, acc)
        back_mesh, back_sub = react_ghost(at)(*rows)
        (force,) = react_own(at)(*rows)
        back_mesh = shifted(back_mesh, "mesh", -1)
        back_sub = shifted(back_sub, "sub", -1)
        args = (own, force, slave, back_mesh, back_sub, mass, mesh_ids, sub_ids)
        if step < STEPS - 1:
            own, to_mesh, to_sub = update(*args)
        else:
            (own,) = finish(*args)
    return own, stress_now.reshape(3, elems)


def solution(mesh):
    return jax.shard_map(
        per_device,
        mesh=mesh,
        in_specs=(
            P(None, ("mesh", "sub")),
            P(None, ("mesh", "sub")),
            P(("mesh", "sub")),
            P(None, ("mesh", "sub")),
            P(None, ("mesh", "sub")),
            P(("mesh", "sub")),
            P(("mesh", "sub")),
            P(None, ("mesh", "sub")),
            P(None, None, ("mesh", "sub")),
            P(None, None, ("mesh", "sub")),
        ),
        out_specs=(P(None, ("mesh", "sub")), P(None, ("mesh", "sub"))),
        check_vma=False,
    )
```

```python
import functools
import math

import jax
import jax.numpy as jnp
from jax import lax
from jax.experimental import pallas as pl
from jax.experimental.pallas import tpu as pltpu
from jax.sharding import PartitionSpec as P


SEG = 128
STEPS = 4
LOW = 256
ROWS = 8
SENT = 6
UNROLL = 8

TIME_STEP = 0.2
YOUNG = 1.0
POISSON = 0.3
HOURGLASS = 0.01
PENALTY = 0.2
REACH = 4.0
HOUR_SIGNS = (1.0, -1.0, 1.0, -1.0)

F32 = jnp.float32
BF16 = jnp.bfloat16


def shifted(value, axis, steps):
    count = lax.axis_size(axis)
    pairs = [(source, (source + steps) % count) for source in range(count)]
    return lax.ppermute(value, axis, pairs)


def split_two(value):
    high = value.astype(BF16).astype(F32)
    return high, value - high


def split_three(value):
    high = value.astype(BF16).astype(F32)
    rest = value - high
    mid = rest.astype(BF16).astype(F32)
    return high, mid, rest - mid


def one_hot_low(low_ids, low=LOW):
    width = low_ids.shape[1]
    rows = lax.broadcasted_iota(jnp.int32, (low, width), 0)
    return jnp.where(rows == low_ids, 1.0, 0.0).astype(BF16)


def stack_columns(rows_eight):
    count = rows_eight.shape[1] // LOW
    return jnp.concatenate(
        [rows_eight[:, part * LOW : (part + 1) * LOW] for part in range(count)], axis=0
    )


def pick_high(product, high_ids, count):
    width = product.shape[1]
    total = jnp.zeros((ROWS, width), F32)
    for part in range(count):
        total = jnp.where(high_ids == part, product[part * ROWS : (part + 1) * ROWS], total)
    return total


def split_rows(three):
    high, low = split_two(three)
    pad = jnp.zeros((ROWS - 6, three.shape[1]), F32)
    return jnp.concatenate([high, low, pad], axis=0)


def corner_ids(conn_ref, block):
    return conn_ref[:, pl.ds(pl.multiple_of(block * SEG, SEG), SEG)]


def pair_row(ids, half):
    return jnp.concatenate([ids[2 * half : 2 * half + 1], ids[2 * half + 1 : 2 * half + 2]], axis=1)


def pair_lanes(ids, half):
    rows = [jnp.broadcast_to(ids[2 * half + i : 2 * half + i + 1], (4, SEG)) for i in range(2)]
    return jnp.concatenate(rows, axis=0)


def gather_tiles(table, conn_ref, out_ref):
    count = table.shape[0] // ROWS

    def tile(block, carry):
        corners = corner_ids(conn_ref, block)
        for half in range(2):
            ids = pair_row(corners, half)
            product = jnp.dot(table, one_hot_low(ids & (LOW - 1)), preferred_element_type=F32)
            total = pick_high(product, ids >> 8, count)
            for i in range(2):
                start = pl.multiple_of((block * 4 + half * 2 + i) * ROWS, ROWS)
                out_ref[pl.ds(start, ROWS), :] = total[:, i * SEG : (i + 1) * SEG]
        return carry

    lax.fori_loop(0, conn_ref.shape[1] // SEG, tile, 0, unroll=UNROLL // 2)


def cross(left, right):
    return (
        left[1] * right[2] - left[2] * right[1],
        left[2] * right[0] - left[0] * right[2],
        left[0] * right[1] - left[1] * right[0],
    )


def sub3(left, right):
    return tuple(a - b for a, b in zip(left, right))


def dot3(left, right):
    return left[0] * right[0] + left[1] * right[1] + left[2] * right[2]


def geometry(corner):
    raw = cross(sub3(corner[2], corner[0]), sub3(corner[3], corner[1]))
    twice_area = jnp.maximum(jnp.sqrt(dot3(raw, raw)), 1.0)
    inverse = 1.0 / twice_area
    normal = tuple(part * inverse for part in raw)
    centre = tuple(
        0.25 * (corner[0][c] + corner[1][c] + corner[2][c] + corner[3][c]) for c in range(3)
    )
    return centre, normal, twice_area, inverse


def corner_rows(ref, group, component):
    return [
        ref[pl.ds((group * 32 + corner) * ROWS + component, 8, stride=4 * ROWS), :]
        for corner in range(4)
    ]


def tree_pick(values, bits):
    level = 0
    while len(values) > 1:
        values = [
            jnp.where(bits[level], values[i + 1], values[i]) if i + 1 < len(values) else values[i]
            for i in range(0, len(values), 2)
        ]
        level += 1
    return values[0]


def fill_chunks(three, chunk_ref, first):
    four = jnp.concatenate([three, jnp.zeros((1, three.shape[1]), F32)], axis=0)
    twice = jnp.concatenate([four, four], axis=0)
    for part in range(three.shape[1] // SEG):
        chunk_ref[first + part] = twice[:, part * SEG : (part + 1) * SEG]


def lane_pick(chunk_ref, ids, high_ids):
    count = chunk_ref.shape[0]
    low_ids = ids & (SEG - 1)
    bits = [((high_ids >> bit) & 1) == 1 for bit in range((count - 1).bit_length())]
    values = [
        jnp.take_along_axis(chunk_ref[part], low_ids, axis=1, mode="promise_in_bounds")
        for part in range(count)
    ]
    return tree_pick(values, bits)


def own_rows_kernel(own_ref, conn_ref, rows_ref, chunk_ref):
    fill_chunks(own_ref[0:3, :], chunk_ref, 0)

    def tile(block, carry):
        corners = corner_ids(conn_ref, block)
        for half in range(2):
            ids = pair_lanes(corners, half)
            start = pl.multiple_of((block * 2 + half) * ROWS, ROWS)
            rows_ref[pl.ds(start, ROWS), :] = lane_pick(chunk_ref, ids, ids >> 7)
        return carry

    lax.fori_loop(0, conn_ref.shape[1] // SEG, tile, 0, unroll=4)


def geometry_kernel(
    step, nodes, picks_any, mesh_ref, sub_ref, conn_ref, own_rows_ref, corner_ref, geo_ref,
    out_ref, kept_ref, rows_ref, chunk_ref, picks_ref, sem,
):
    fetch = pltpu.make_async_copy(picks_any, picks_ref, sem)
    fetch.start()
    blocks = geo_ref.shape[0] // ROWS
    first = mesh_ref.shape[1] // SEG
    fill_chunks(mesh_ref[0:3, :], chunk_ref, 0)
    fill_chunks(sub_ref[0:3, :], chunk_ref, first)

    def tile(block, carry):
        corners = corner_ids(conn_ref, block)
        for half in range(2):
            ids = pair_lanes(corners, half)
            start = pl.multiple_of((block * 2 + half) * ROWS, ROWS)
            far = lane_pick(chunk_ref, ids, (ids >> 7) - nodes // SEG)
            near = own_rows_ref[pl.ds(start, ROWS), :]
            rows_ref[pl.ds(start, ROWS), :] = jnp.where(ids >= nodes, far, near)
        return carry

    lax.fori_loop(0, conn_ref.shape[1] // SEG, tile, 0, unroll=32)
    for group in range(blocks // 8):
        corner = [
            tuple(rows_ref[pl.ds(group * 128 + i * 4 + c, 8, stride=16), :] for c in range(3))
            for i in range(4)
        ]
        for i in range(4):
            for c in range(3):
                corner_ref[i * 3 + c, group * 8 : (group + 1) * 8, :] = corner[i][c]
        centre, normal, _, _ = geometry(corner)
        for c in range(3):
            geo_ref[pl.ds(group * 8 * ROWS + c, 8, stride=ROWS), :] = centre[c]
            geo_ref[pl.ds(group * 8 * ROWS + 3 + c, 8, stride=ROWS), :] = normal[c]
        for c in range(6, ROWS):
            geo_ref[pl.ds(group * 8 * ROWS + c, 8, stride=ROWS), :] = jnp.zeros((8, SEG), F32)

    fetch.wait()
    peers, groups = out_ref.shape[:2]
    per_peer = picks_ref.shape[1] // peers
    for peer in range(peers):
        rows = []
        for slot in range(peer * per_peer, (peer + 1) * per_peer):
            start = pl.multiple_of(picks_ref[step, slot] * ROWS, ROWS)
            block = geo_ref[pl.ds(start, ROWS), :]
            rows.append(block[:SENT])
            if kept_ref is not None:
                kept_ref[slot * ROWS : (slot + 1) * ROWS, :] = block
        rows.append(jnp.zeros((groups * 4 - per_peer * SENT, SEG), F32))
        rows = jnp.concatenate([part for part in rows if part.shape[0]], axis=0)
        for group in range(groups):
            out_ref[peer, group] = rows[group * 4 : (group + 1) * 4]


def geometry_slots_kernel(step, nodes, *refs):
    ins, (corner_ref, kept_ref, out_ref), (geo_ref, *scratch) = refs[:5], refs[5:8], refs[8:]
    geometry_kernel(step, nodes, *ins, corner_ref, geo_ref, out_ref, kept_ref, *scratch)


def geometry_blocks_kernel(step, nodes, *refs):
    geometry_kernel(step, nodes, *refs[:8], None, *refs[8:])


def force_kernel(
    own_ref, mesh_ref, sub_ref, conn_ref, corner_ref, stress_ref, push_ref, new_ref, rows_ref
):
    blocks = corner_ref.shape[1]
    full = jnp.concatenate([own_ref[3:6, :], mesh_ref[3:6, :], sub_ref[3:6, :]], axis=1)
    gather_tiles(stack_columns(split_rows(full)).astype(BF16), conn_ref, rows_ref)
    stiff = YOUNG / (1.0 - POISSON * POISSON)
    for group in range(blocks // 8):
        here = slice(group * 8, (group + 1) * 8)
        speed_parts = []
        for component in range(3):
            high = corner_rows(rows_ref, group, component)
            low = corner_rows(rows_ref, group, component + 3)
            speed_parts.append([a + b for a, b in zip(high, low)])
        speed = [tuple(speed_parts[c][i] for c in range(3)) for i in range(4)]
        corner = [tuple(corner_ref[i * 3 + c, here, :] for c in range(3)) for i in range(4)]
        centre, normal, twice_area, inverse = geometry(corner)
        side = sub3(corner[1], corner[0])
        side_inverse = 1.0 / jnp.maximum(jnp.sqrt(dot3(side, side)), 1.0)
        axis_one = tuple(part * side_inverse for part in side)
        axis_two = cross(normal, axis_one)
        relative = [sub3(corner[i], centre) for i in range(4)]
        x = [dot3(relative[i], axis_one) for i in range(4)]
        y = [dot3(relative[i], axis_two) for i in range(4)]
        u = [dot3(speed[i], axis_one) for i in range(4)]
        v = [dot3(speed[i], axis_two) for i in range(4)]
        y13, y20 = (y[1] - y[3]) * inverse, (y[2] - y[0]) * inverse
        x31, x02 = (x[3] - x[1]) * inverse, (x[0] - x[2]) * inverse
        bx = [y13, y20, -y13, -y20]
        by = [x31, x02, -x31, -x02]
        u02, u13, v02, v13 = u[0] - u[2], u[1] - u[3], v[0] - v[2], v[1] - v[3]
        rate_xx = y13 * u02 + y20 * u13
        rate_yy = x31 * v02 + x02 * v13
        rate_xy = x31 * u02 + x02 * u13 + y13 * v02 + y20 * v13
        s0 = stress_ref[0, here, :] + TIME_STEP * (stiff * (rate_xx + POISSON * rate_yy))
        s1 = stress_ref[1, here, :] + TIME_STEP * (stiff * (POISSON * rate_xx + rate_yy))
        s2 = stress_ref[2, here, :] + TIME_STEP * (YOUNG / (2.0 * (1.0 + POISSON)) * rate_xy)
        new_ref[0, here, :] = s0
        new_ref[1, here, :] = s1
        new_ref[2, here, :] = s2
        half_area = 0.5 * twice_area
        hour_x = x[0] - x[1] + x[2] - x[3]
        hour_y = y[0] - y[1] + y[2] - y[3]
        shape = [HOUR_SIGNS[i] - hour_x * bx[i] - hour_y * by[i] for i in range(4)]
        rate = tuple(
            HOURGLASS * sum(shape[i] * speed[i][c] for i in range(4)) for c in range(3)
        )
        for i in range(4):
            force_x = half_area * (bx[i] * s0 + by[i] * s2)
            force_y = half_area * (by[i] * s1 + bx[i] * s2)
            start = (group * 32 + i) * ROWS
            for c in range(3):
                internal = force_x * axis_one[c] + force_y * axis_two[c] + shape[i] * rate[c]
                high, low = split_two(-internal)
                push_ref[pl.ds(start + c, 8, stride=4 * ROWS), :] = high
                push_ref[pl.ds(start + 3 + c, 8, stride=4 * ROWS), :] = low
            for c in range(6, ROWS):
                push_ref[pl.ds(start + c, 8, stride=4 * ROWS), :] = jnp.zeros((8, SEG), F32)


def product_tiles(value, turn):
    parts = split_three(value)
    order = (0, 0, 1, 0, 1, 2) if turn else (0, 1, 0, 2, 1, 0)
    return [parts[index] for index in order]


def row_mix(three, extras):
    width = three.shape[1]
    rows = [three] + extras
    pad = -sum(part.shape[0] for part in rows) % ROWS
    if pad:
        rows.append(jnp.zeros((pad, width), F32))
    return jnp.concatenate(rows, axis=0)


def node_features(place):
    ones = jnp.ones((3, place.shape[1]), F32)
    square = jnp.concatenate(
        split_three(place[0:1] ** 2 + place[1:2] ** 2 + place[2:3] ** 2), axis=0
    )
    tiles = product_tiles(place, True)
    return row_mix(tiles[0], tiles[1:] + [ones]), row_mix(tiles[0], tiles[1:] + [ones, square])


def segment_features(centre, normal):
    ones = jnp.ones((3, centre.shape[1]), F32)
    lean = centre[0:1] * normal[0:1] + centre[1:2] * normal[1:2] + centre[2:3] * normal[2:3]
    lean = jnp.concatenate(split_three(-lean), axis=0)
    square = centre[0:1] ** 2 + centre[1:2] ** 2 + centre[2:3] ** 2
    square = jnp.concatenate(split_three(square), axis=0)
    tiles = product_tiles(normal, False)
    gap = row_mix(tiles[0], tiles[1:] + [lean])
    tiles = product_tiles(-2.0 * centre, False)
    return gap, row_mix(tiles[0], tiles[1:] + [square, ones])


FEATURES = 6 * ROWS
SCALE = math.sqrt(math.log2(math.e) / REACH)


def feature_kernel(step, own_ref, mask_ref, node_ref):
    cands = mask_ref.shape[1]

    def features(index, carry):
        start = pl.multiple_of(index * SEG, SEG)
        gap, far = node_features(own_ref[0:3, pl.ds(start, SEG)] * SCALE)
        mask = mask_ref[step, :, pl.ds(start, SEG)].astype(F32)
        for k in range(cands):
            live = mask[k : k + 1]
            rows = jnp.concatenate([gap * live, far], axis=0)
            rows = jnp.concatenate([rows, jnp.zeros((SEG - FEATURES, SEG), F32)], axis=0)
            node_ref[k, pl.ds(start, SEG), :] = rows.T.astype(BF16)
        return carry

    lax.fori_loop(0, own_ref.shape[1] // SEG, features, 0, unroll=2)


def contact_kernel(
    step, list_any, node_ref, slots_ref, force_ref, react_ref, seg_ref, push_ref, list_ref, sem
):
    fetch = pltpu.make_async_copy(list_any, list_ref, sem)
    fetch.start()
    buckets = node_ref.shape[1] // SEG
    cands = node_ref.shape[0]
    slots = react_ref.shape[0]
    react_ref[...] = jnp.zeros_like(react_ref)

    peers, groups = slots_ref.shape[:2]
    per_peer = slots // peers
    for index in range(slots):
        if index % per_peer == 0:
            rows = [slots_ref[index // per_peer, group] for group in range(groups)]
            rows = jnp.concatenate(rows, axis=0)
        tile = rows[index % per_peer * SENT : (index % per_peer + 1) * SENT]
        gap, far = segment_features(tile[0:3] * SCALE, tile[3:6])
        blank = jnp.zeros((FEATURES // 2, SEG), F32)
        left = jnp.concatenate([gap, blank], axis=0)
        right = jnp.concatenate([blank, far], axis=0)
        seg_ref[index] = jnp.concatenate([left, right], axis=1).astype(BF16)
        push = split_rows(tile[3:6])
        push = jnp.concatenate([push, push], axis=1)
        push_ref[index] = jnp.concatenate([push, jnp.zeros_like(push)], axis=0).astype(BF16)
    fetch.wait()

    def bucket(index, carry):
        start = pl.multiple_of(index * SEG, SEG)
        chosen = [list_ref[step, k, index] for k in range(cands)]
        pairs = [
            jnp.dot(
                node_ref[k, pl.ds(start, SEG), :][:, :FEATURES],
                seg_ref[chosen[k]],
                preferred_element_type=F32,
            )
            for k in range(cands)
        ]
        parts = []
        for k in range(cands):
            gap, far = pairs[k][:, :SEG], pairs[k][:, SEG:]
            weight = jnp.minimum(gap, 0.0) * jnp.exp2(gap * gap - far)
            react_ref[pl.ds(chosen[k], 1), :] += jnp.sum(weight, axis=0, keepdims=True)
            high = weight.astype(BF16)
            low = (weight - high.astype(F32)).astype(BF16)
            parts.append(jnp.concatenate([high, low], axis=1))
        total = dot_rows(
            jnp.concatenate([push_ref[slot] for slot in chosen], axis=1),
            jnp.concatenate(parts, axis=1),
        )
        force = (total[0:3] + total[3:6]) * (-PENALTY / SCALE)
        force_ref[:, pl.ds(start, SEG)] = row_mix(force, [])
        return carry

    lax.fori_loop(0, buckets, bucket, 0, unroll=16)
    react_ref[...] = react_ref[...] * (-PENALTY / SCALE)


def internal_kernel(rows_ref, conn_ref, acc_ref):
    scatter_tiles(rows_ref, conn_ref, acc_ref)


def pick_kernel(picks_ref, conn_ref, tiles_ref):
    for step in range(tiles_ref.shape[0]):

        def copy(slot, carry):
            tiles_ref[step, slot] = corner_ids(conn_ref, picks_ref[step, slot])
            return carry

        lax.fori_loop(0, tiles_ref.shape[1], copy, 0, unroll=8)


def collect_kernel(step, picks_ref, back_ref, seg_ref):
    seg_ref[...] = jnp.zeros_like(seg_ref)

    def collect(slot, carry):
        seg_ref[pl.ds(picks_ref[step, slot], 1), :] += back_ref[pl.ds(slot, 1), :]
        return carry

    lax.fori_loop(0, back_ref.shape[0], collect, 0)


def react_tiles(step, first, last, low, unroll, blocks_ref, back_ref, tiles_ref):
    def tile(index, total):
        react = back_ref[pl.ds(index, 1), :]
        normal = blocks_ref[pl.ds(pl.multiple_of(index * ROWS, ROWS), ROWS), :][3:6]
        rows = split_rows(-0.25 * react * normal)
        values = jnp.concatenate([rows, rows], axis=1)
        corners = tiles_ref[step, index]
        for half in range(2):
            ids = pair_row(corners, half)
            spread = spread_rows(values, ids, first, last, low)
            total = total + dot_rows(spread, one_hot_low(ids & (low - 1), low))
        return total

    start = jnp.zeros(((last - first) * ROWS, low), F32)
    return lax.fori_loop(0, back_ref.shape[0], tile, start, unroll=unroll)


def unstack(total):
    count = total.shape[0] // ROWS
    full = jnp.concatenate(
        [total[part * ROWS : (part + 1) * ROWS] for part in range(count)], axis=1
    )
    return row_mix(full[0:3] + full[3:6], [])


def react_ghost_kernel(step, blocks_ref, back_ref, tiles_ref, acc_ref, mesh_ref, sub_ref):
    count = acc_ref.shape[0] // ROWS
    ghosts = mesh_ref.shape[1] + sub_ref.shape[1]
    first, last = count * LOW // SEG - ghosts // SEG, count * LOW // SEG
    total = react_tiles(step, first, last, SEG, 16, blocks_ref, back_ref, tiles_ref)
    full = unstack(total) + unstack(acc_ref[(count - ghosts // LOW) * ROWS :, :])
    mesh_ref[...] = full[:, : mesh_ref.shape[1]]
    sub_ref[...] = full[:, mesh_ref.shape[1] :]


def react_own_kernel(step, blocks_ref, back_ref, tiles_ref, acc_ref, own_ref):
    nodes = own_ref.shape[1]
    total = react_tiles(step, 0, nodes // SEG, SEG, 16, blocks_ref, back_ref, tiles_ref)
    own_ref[...] = unstack(total) + unstack(acc_ref[: nodes // LOW * ROWS, :])


def spread_rows(values, ids, first, last, low=LOW):
    width = values.shape[1]
    twice = jnp.concatenate([values, values], axis=0).astype(BF16)
    high_ids = jnp.broadcast_to((ids >> (low.bit_length() - 1)).astype(F32), (2 * ROWS, width))
    second = lax.broadcasted_iota(jnp.int32, (2 * ROWS, width), 0) >= ROWS
    offset = (high_ids - jnp.where(second, 1.0, 0.0)).astype(BF16)
    zero = jnp.zeros((), BF16)
    parts = [
        jnp.where(offset == jnp.asarray(part, BF16), twice, zero) for part in range(first, last, 2)
    ]
    return jnp.concatenate(parts, axis=0)


def dot_rows(left, right):
    return lax.dot_general(left, right, (((1,), (1,)), ((), ())), preferred_element_type=F32)


def scatter_tiles(rows_ref, conn_ref, acc_ref):
    count = acc_ref.shape[0] // ROWS
    acc_ref[...] = jnp.zeros_like(acc_ref)

    def tile(block, carry):
        corners = corner_ids(conn_ref, block)
        for half in range(2):
            ids = pair_row(corners, half)
            start = pl.multiple_of((block * 2 + half) * 2 * ROWS, 2 * ROWS)
            parts = [rows_ref[pl.ds(start + i * ROWS, ROWS), :] for i in range(2)]
            spread = spread_rows(jnp.concatenate(parts, axis=1), ids, 0, count)
            acc_ref[...] += dot_rows(spread, one_hot_low(ids & (LOW - 1)))
        return carry

    lax.fori_loop(0, conn_ref.shape[1] // SEG, tile, 0, unroll=UNROLL // 2)


def add_back(back, ids_ref, count):
    rows = split_rows(back[0:3])
    total = jnp.zeros((count * ROWS, SEG), F32)
    for index in range(back.shape[1] // LOW):
        here = slice(index * LOW, (index + 1) * LOW)
        ids = ids_ref[:, here]
        spread = spread_rows(rows[:, here], ids, 0, count, SEG)
        total = total + dot_rows(spread, one_hot_low(ids & (SEG - 1), SEG))
    return total


def pack_ghosts(table, ids_ref, out_ref):
    count = table.shape[0] // (3 * ROWS)
    size = count * ROWS
    for index in range(out_ref.shape[1] // LOW):
        here = slice(index * LOW, (index + 1) * LOW)
        ids = ids_ref[:, here]
        product = jnp.dot(table, one_hot_low(ids & (LOW - 1)), preferred_element_type=F32)
        product = product[:size] + product[size : 2 * size] + product[2 * size :]
        out_ref[:, here] = pick_high(product, ids >> 8, count)


def pack_both(own, mesh_ids_ref, sub_ids_ref, to_mesh_ref, to_sub_ref):
    parts = [stack_columns(part) for part in split_three(own)]
    table = jnp.concatenate(parts, axis=0).astype(BF16)
    pack_ghosts(table, mesh_ids_ref, to_mesh_ref)
    pack_ghosts(table, sub_ids_ref, to_sub_ref)


def pack_kernel(
    coords_any, veloc_any, mesh_any, sub_any, own_ref, to_mesh_ref, to_sub_ref, coords_ref,
    veloc_ref, mesh_ids_ref, sub_ids_ref, sems,
):
    sources = (coords_any, veloc_any, mesh_any, sub_any)
    targets = (coords_ref, veloc_ref, mesh_ids_ref, sub_ids_ref)
    copies = [
        pltpu.make_async_copy(source, target, sems.at[index])
        for index, (source, target) in enumerate(zip(sources, targets))
    ]
    for copy in copies:
        copy.start()
    for copy in copies:
        copy.wait()
    pad = jnp.zeros((ROWS - 6, coords_ref.shape[1]), F32)
    own = jnp.concatenate([coords_ref[...], veloc_ref[...], pad], axis=0)
    own_ref[...] = own
    pack_both(own, mesh_ids_ref, sub_ids_ref, to_mesh_ref, to_sub_ref)


def new_state(
    own_ref, force_ref, slave_ref, back_mesh_ref, back_sub_ref, mass_ref, mesh_ids_ref,
    sub_ids_ref,
):
    count = own_ref.shape[1] // SEG
    extra = add_back(back_mesh_ref[...], mesh_ids_ref, count) + add_back(
        back_sub_ref[...], sub_ids_ref, count
    )
    full = unstack(extra)
    force = force_ref[0:3, :] + slave_ref[0:3, :] + full[0:3]
    return own_ref[3:6, :] + TIME_STEP * force / mass_ref[...]


def update_kernel(*refs):
    own_ref, mesh_ids_ref, sub_ids_ref = refs[0], refs[6], refs[7]
    new_ref, to_mesh_ref, to_sub_ref = refs[8:]
    speed = new_state(*refs[:8])
    place = own_ref[0:3, :] + TIME_STEP * speed
    own = jnp.concatenate([place, speed, jnp.zeros((ROWS - 6, place.shape[1]), F32)], axis=0)
    new_ref[...] = own
    pack_both(own, mesh_ids_ref, sub_ids_ref, to_mesh_ref, to_sub_ref)


def last_kernel(*refs):
    refs[8][...] = new_state(*refs[:8])


VM = pl.BlockSpec(memory_space=pltpu.VMEM)
SM = pl.BlockSpec(memory_space=pltpu.SMEM)
ANY = pl.BlockSpec(memory_space=pl.ANY)
HBM = pl.BlockSpec(memory_space=pltpu.HBM)


def call(kernel, outs, ins, scratch=(), flops=0):
    shapes = tuple(
        jax.ShapeDtypeStruct(shape, F32) if isinstance(shape, tuple) else shape for shape in outs
    )
    return pl.pallas_call(
        kernel,
        out_shape=shapes,
        in_specs=list(ins),
        out_specs=tuple(VM for _ in outs),
        scratch_shapes=[
            pltpu.VMEM(shape, F32) if isinstance(shape, tuple) else shape for shape in scratch
        ],
        compiler_params=pltpu.CompilerParams(vmem_limit_bytes=8 << 20),
        cost_estimate=pl.CostEstimate(flops=flops, bytes_accessed=1 << 20, transcendentals=0),
    )


def per_device(
    coords,
    veloc,
    node_mass,
    stress,
    connect,
    send_mesh,
    send_sub,
    send_pick,
    bucket_list,
    pair_mask,
):
    nodes = coords.shape[1]
    elems = stress.shape[1]
    ghost_mesh = send_mesh.shape[0]
    ghost_sub = send_sub.shape[0]
    width = nodes + ghost_mesh + ghost_sub
    peers = lax.axis_size("mesh")
    slots = send_pick.shape[1]
    per_peer = slots // peers
    blocks = elems // SEG
    mesh_ids = send_mesh.reshape(1, ghost_mesh)
    sub_ids = send_sub.reshape(1, ghost_sub)
    mass = node_mass.reshape(1, nodes)
    stress_now = stress.reshape(3, blocks, SEG)
    conn = connect

    chunks = nodes // SEG
    ghost_chunks = (ghost_mesh + ghost_sub) // SEG
    cands = bucket_list.shape[1]

    pack = call(
        pack_kernel,
        [
            (ROWS, nodes),
            (ROWS, ghost_mesh),
            (ROWS, ghost_sub),
        ],
        [HBM] * 4,
        [
            (3, nodes),
            (3, nodes),
            pltpu.VMEM((1, ghost_mesh), jnp.int32),
            pltpu.VMEM((1, ghost_sub), jnp.int32),
            pltpu.SemaphoreType.DMA((4,)),
        ],
    )
    own_rows_of = call(
        own_rows_kernel, [(2 * blocks * ROWS, SEG)], [VM] * 2, [(chunks, ROWS, SEG)], flops=1 << 31
    )
    by_slot = slots <= blocks
    geom = lambda step: call(
        functools.partial(
            geometry_slots_kernel if by_slot else geometry_blocks_kernel, step, nodes
        ),
        [
            (12, blocks, SEG),
            (slots * ROWS if by_slot else blocks * ROWS, SEG),
            (peers, pl.cdiv(per_peer * SENT, 4), 4, SEG),
        ],
        [ANY] + [VM] * 4,
        ([(blocks * ROWS, SEG)] if by_slot else [])
        + [
            (2 * blocks * ROWS, SEG),
            (ghost_chunks, ROWS, SEG),
            pltpu.SMEM(send_pick.shape, jnp.int32),
            pltpu.SemaphoreType.DMA,
        ],
        flops=1 << 30,
    )
    forces = call(
        force_kernel,
        [(4 * blocks * ROWS, SEG), (3, blocks, SEG)],
        [VM] * 6,
        [(4 * blocks * ROWS, SEG)],
        flops=1 << 31,
    )
    features = lambda step: call(
        functools.partial(feature_kernel, step),
        [jax.ShapeDtypeStruct((cands, nodes, SEG), BF16)],
        [VM] * 2,
        flops=1 << 30,
    )
    contact = lambda step: call(
        functools.partial(contact_kernel, step),
        [(ROWS, nodes), (slots, SEG)],
        [ANY] + [VM] * 2,
        [
            pltpu.VMEM((slots, FEATURES, 2 * SEG), BF16),
            pltpu.VMEM((slots, 2 * ROWS, 2 * SEG), BF16),
            pltpu.SMEM(bucket_list.shape, jnp.int32),
            pltpu.SemaphoreType.DMA,
        ],
        flops=1 << 31,
    )
    internal_of = call(internal_kernel, [(width // LOW * ROWS, LOW)], [VM] * 2, flops=1 << 31)
    react_ghost = lambda step: call(
        functools.partial(react_ghost_kernel, step),
        [(ROWS, ghost_mesh), (ROWS, ghost_sub)],
        [VM] * 4,
        flops=1 << 29,
    )
    react_own = lambda step: call(
        functools.partial(react_own_kernel, step), [(ROWS, nodes)], [VM] * 4, flops=1 << 30
    )
    update = call(update_kernel, [(ROWS, nodes), (ROWS, ghost_mesh), (ROWS, ghost_sub)], [VM] * 8)
    finish = call(last_kernel, [(3, nodes)], [VM] * 8)

    pick_tiles = call(
        pick_kernel,
        [jax.ShapeDtypeStruct((STEPS, slots, 4, SEG), jnp.int32)],
        [SM, VM],
        flops=1 << 20,
    )
    collect = lambda step: call(functools.partial(collect_kernel, step), [(blocks, SEG)], [SM, VM])

    own, to_mesh, to_sub = pack(
        *[
            pltpu.with_memory_space_constraint(source, pltpu.HBM)
            for source in (coords, veloc, mesh_ids, sub_ids)
        ]
    )
    if by_slot:
        (tiles,) = pick_tiles(send_pick, conn)
    else:
        tiles = conn.reshape(4, blocks, SEG).transpose(1, 0, 2)[None]
    for step in range(STEPS):
        from_mesh = shifted(to_mesh, "mesh", 1)
        from_sub = shifted(to_sub, "sub", 1)
        (own_rows,) = own_rows_of(own, conn)
        (node,) = features(step)(own, pair_mask)
        corner, kept, outgoing = geom(step)(
            send_pick, from_mesh, from_sub, conn, own_rows
        )
        incoming = lax.all_to_all(
            outgoing, "mesh", split_axis=0, concat_axis=0, tiled=True
        )
        pushes, stress_now = forces(own, from_mesh, from_sub, conn, corner, stress_now)
        slave, react = contact(step)(bucket_list, node, incoming)
        returned = lax.all_to_all(
            react.reshape(peers, per_peer, SEG),
            "mesh", split_axis=0, concat_axis=0, tiled=True,
        ).reshape(slots, SEG)
        (acc,) = internal_of(pushes, conn)
        at = step if by_slot else 0
        if by_slot:
            rows = (kept, returned, tiles, acc)
        else:
            rows = (kept, collect(step)(send_pick, returned)[0], tiles, acc)
        back_mesh, back_sub = react_ghost(at)(*rows)
        (force,) = react_own(at)(*rows)
        back_mesh = shifted(back_mesh, "mesh", -1)
        back_sub = shifted(back_sub, "sub", -1)
        args = (own, force, slave, back_mesh, back_sub, mass, mesh_ids, sub_ids)
        if step < STEPS - 1:
            own, to_mesh, to_sub = update(*args)
        else:
            (own,) = finish(*args)
    return own, stress_now.reshape(3, elems)


def solution(mesh):
    return jax.shard_map(
        per_device,
        mesh=mesh,
        in_specs=(
            P(None, ("mesh", "sub")),
            P(None, ("mesh", "sub")),
            P(("mesh", "sub")),
            P(None, ("mesh", "sub")),
            P(None, ("mesh", "sub")),
            P(("mesh", "sub")),
            P(("mesh", "sub")),
            P(None, ("mesh", "sub")),
            P(None, None, ("mesh", "sub")),
            P(None, None, ("mesh", "sub")),
        ),
        out_specs=(P(None, ("mesh", "sub")), P(None, ("mesh", "sub"))),
        check_vma=False,
    )
```

```python
import functools
import math

import jax
import jax.numpy as jnp
from jax import lax
from jax.experimental import pallas as pl
from jax.experimental.pallas import tpu as pltpu
from jax.sharding import PartitionSpec as P


SEG = 128
STEPS = 4
LOW = 256
ROWS = 8
SENT = 6
UNROLL = 8

TIME_STEP = 0.2
YOUNG = 1.0
POISSON = 0.3
HOURGLASS = 0.01
PENALTY = 0.2
REACH = 4.0
HOUR_SIGNS = (1.0, -1.0, 1.0, -1.0)

F32 = jnp.float32
BF16 = jnp.bfloat16


def shifted(value, axis, steps):
    count = lax.axis_size(axis)
    pairs = [(source, (source + steps) % count) for source in range(count)]
    return lax.ppermute(value, axis, pairs)


def split_two(value):
    high = value.astype(BF16).astype(F32)
    return high, value - high


def split_three(value):
    high = value.astype(BF16).astype(F32)
    rest = value - high
    mid = rest.astype(BF16).astype(F32)
    return high, mid, rest - mid


def one_hot_low(low_ids, low=LOW):
    width = low_ids.shape[1]
    rows = lax.broadcasted_iota(jnp.int32, (low, width), 0)
    return jnp.where(rows == low_ids, 1.0, 0.0).astype(BF16)


def stack_columns(rows_eight):
    count = rows_eight.shape[1] // LOW
    return jnp.concatenate(
        [rows_eight[:, part * LOW : (part + 1) * LOW] for part in range(count)], axis=0
    )


def pick_high(product, high_ids, count):
    width = product.shape[1]
    total = jnp.zeros((ROWS, width), F32)
    for part in range(count):
        total = jnp.where(high_ids == part, product[part * ROWS : (part + 1) * ROWS], total)
    return total


def split_rows(three):
    high, low = split_two(three)
    pad = jnp.zeros((ROWS - 6, three.shape[1]), F32)
    return jnp.concatenate([high, low, pad], axis=0)


def corner_ids(conn_ref, block):
    return conn_ref[:, pl.ds(pl.multiple_of(block * SEG, SEG), SEG)]


def pair_row(ids, half):
    return jnp.concatenate([ids[2 * half : 2 * half + 1], ids[2 * half + 1 : 2 * half + 2]], axis=1)


def pair_lanes(ids, half):
    rows = [jnp.broadcast_to(ids[2 * half + i : 2 * half + i + 1], (4, SEG)) for i in range(2)]
    return jnp.concatenate(rows, axis=0)


def gather_tiles(table, conn_ref, out_ref):
    count = table.shape[0] // ROWS

    def tile(block, carry):
        corners = corner_ids(conn_ref, block)
        for half in range(2):
            ids = pair_row(corners, half)
            product = jnp.dot(table, one_hot_low(ids & (LOW - 1)), preferred_element_type=F32)
            total = pick_high(product, ids >> 8, count)
            for i in range(2):
                start = pl.multiple_of((block * 4 + half * 2 + i) * ROWS, ROWS)
                out_ref[pl.ds(start, ROWS), :] = total[:, i * SEG : (i + 1) * SEG]
        return carry

    lax.fori_loop(0, conn_ref.shape[1] // SEG, tile, 0, unroll=UNROLL // 2)


def cross(left, right):
    return (
        left[1] * right[2] - left[2] * right[1],
        left[2] * right[0] - left[0] * right[2],
        left[0] * right[1] - left[1] * right[0],
    )


def sub3(left, right):
    return tuple(a - b for a, b in zip(left, right))


def dot3(left, right):
    return left[0] * right[0] + left[1] * right[1] + left[2] * right[2]


def geometry(corner):
    raw = cross(sub3(corner[2], corner[0]), sub3(corner[3], corner[1]))
    twice_area = jnp.maximum(jnp.sqrt(dot3(raw, raw)), 1.0)
    inverse = 1.0 / twice_area
    normal = tuple(part * inverse for part in raw)
    centre = tuple(
        0.25 * (corner[0][c] + corner[1][c] + corner[2][c] + corner[3][c]) for c in range(3)
    )
    return centre, normal, twice_area, inverse


def corner_rows(ref, group, component):
    return [
        ref[pl.ds((group * 32 + corner) * ROWS + component, 8, stride=4 * ROWS), :]
        for corner in range(4)
    ]


def tree_pick(values, bits):
    level = 0
    while len(values) > 1:
        values = [
            jnp.where(bits[level], values[i + 1], values[i]) if i + 1 < len(values) else values[i]
            for i in range(0, len(values), 2)
        ]
        level += 1
    return values[0]


def fill_chunks(three, chunk_ref, first):
    four = jnp.concatenate([three, jnp.zeros((1, three.shape[1]), F32)], axis=0)
    twice = jnp.concatenate([four, four], axis=0)
    for part in range(three.shape[1] // SEG):
        chunk_ref[first + part] = twice[:, part * SEG : (part + 1) * SEG]


def lane_pick(chunk_ref, ids, high_ids):
    count = chunk_ref.shape[0]
    low_ids = ids & (SEG - 1)
    bits = [((high_ids >> bit) & 1) == 1 for bit in range((count - 1).bit_length())]
    values = [
        jnp.take_along_axis(chunk_ref[part], low_ids, axis=1, mode="promise_in_bounds")
        for part in range(count)
    ]
    return tree_pick(values, bits)


def own_rows_kernel(own_ref, conn_ref, rows_ref, chunk_ref):
    fill_chunks(own_ref[0:3, :], chunk_ref, 0)

    def tile(block, carry):
        corners = corner_ids(conn_ref, block)
        for half in range(2):
            ids = pair_lanes(corners, half)
            start = pl.multiple_of((block * 2 + half) * ROWS, ROWS)
            rows_ref[pl.ds(start, ROWS), :] = lane_pick(chunk_ref, ids, ids >> 7)
        return carry

    lax.fori_loop(0, conn_ref.shape[1] // SEG, tile, 0, unroll=4)


def geometry_kernel(
    step, nodes, picks_any, mesh_ref, sub_ref, conn_ref, own_rows_ref, corner_ref, geo_ref,
    out_ref, kept_ref, rows_ref, chunk_ref, picks_ref, sem,
):
    fetch = pltpu.make_async_copy(picks_any, picks_ref, sem)
    fetch.start()
    blocks = geo_ref.shape[0] // ROWS
    first = mesh_ref.shape[1] // SEG
    fill_chunks(mesh_ref[0:3, :], chunk_ref, 0)
    fill_chunks(sub_ref[0:3, :], chunk_ref, first)

    def tile(block, carry):
        corners = corner_ids(conn_ref, block)
        for half in range(2):
            ids = pair_lanes(corners, half)
            start = pl.multiple_of((block * 2 + half) * ROWS, ROWS)
            far = lane_pick(chunk_ref, ids, (ids >> 7) - nodes // SEG)
            near = own_rows_ref[pl.ds(start, ROWS), :]
            rows_ref[pl.ds(start, ROWS), :] = jnp.where(ids >= nodes, far, near)
        return carry

    lax.fori_loop(0, conn_ref.shape[1] // SEG, tile, 0, unroll=32)
    for group in range(blocks // 8):
        corner = [
            tuple(rows_ref[pl.ds(group * 128 + i * 4 + c, 8, stride=16), :] for c in range(3))
            for i in range(4)
        ]
        for i in range(4):
            for c in range(3):
                corner_ref[i * 3 + c, group * 8 : (group + 1) * 8, :] = corner[i][c]
        centre, normal, _, _ = geometry(corner)
        for c in range(3):
            geo_ref[pl.ds(group * 8 * ROWS + c, 8, stride=ROWS), :] = centre[c]
            geo_ref[pl.ds(group * 8 * ROWS + 3 + c, 8, stride=ROWS), :] = normal[c]
        for c in range(6, ROWS):
            geo_ref[pl.ds(group * 8 * ROWS + c, 8, stride=ROWS), :] = jnp.zeros((8, SEG), F32)

    fetch.wait()
    peers, groups = out_ref.shape[:2]
    per_peer = picks_ref.shape[1] // peers
    for peer in range(peers):
        rows = []
        for slot in range(peer * per_peer, (peer + 1) * per_peer):
            start = pl.multiple_of(picks_ref[step, slot] * ROWS, ROWS)
            block = geo_ref[pl.ds(start, ROWS), :]
            rows.append(block[:SENT])
            if kept_ref is not None:
                kept_ref[slot * ROWS : (slot + 1) * ROWS, :] = block
        rows.append(jnp.zeros((groups * 4 - per_peer * SENT, SEG), F32))
        rows = jnp.concatenate([part for part in rows if part.shape[0]], axis=0)
        for group in range(groups):
            out_ref[peer, group] = rows[group * 4 : (group + 1) * 4]


def geometry_slots_kernel(step, nodes, *refs):
    ins, (corner_ref, kept_ref, out_ref), (geo_ref, *scratch) = refs[:5], refs[5:8], refs[8:]
    geometry_kernel(step, nodes, *ins, corner_ref, geo_ref, out_ref, kept_ref, *scratch)


def geometry_blocks_kernel(step, nodes, *refs):
    geometry_kernel(step, nodes, *refs[:8], None, *refs[8:])


def force_kernel(
    own_ref, mesh_ref, sub_ref, conn_ref, corner_ref, stress_ref, push_ref, new_ref, rows_ref
):
    blocks = corner_ref.shape[1]
    full = jnp.concatenate([own_ref[3:6, :], mesh_ref[3:6, :], sub_ref[3:6, :]], axis=1)
    gather_tiles(stack_columns(split_rows(full)).astype(BF16), conn_ref, rows_ref)
    stiff = YOUNG / (1.0 - POISSON * POISSON)
    for group in range(blocks // 8):
        here = slice(group * 8, (group + 1) * 8)
        speed_parts = []
        for component in range(3):
            high = corner_rows(rows_ref, group, component)
            low = corner_rows(rows_ref, group, component + 3)
            speed_parts.append([a + b for a, b in zip(high, low)])
        speed = [tuple(speed_parts[c][i] for c in range(3)) for i in range(4)]
        corner = [tuple(corner_ref[i * 3 + c, here, :] for c in range(3)) for i in range(4)]
        centre, normal, twice_area, inverse = geometry(corner)
        side = sub3(corner[1], corner[0])
        side_inverse = 1.0 / jnp.maximum(jnp.sqrt(dot3(side, side)), 1.0)
        axis_one = tuple(part * side_inverse for part in side)
        axis_two = cross(normal, axis_one)
        relative = [sub3(corner[i], centre) for i in range(4)]
        x = [dot3(relative[i], axis_one) for i in range(4)]
        y = [dot3(relative[i], axis_two) for i in range(4)]
        u = [dot3(speed[i], axis_one) for i in range(4)]
        v = [dot3(speed[i], axis_two) for i in range(4)]
        y13, y20 = (y[1] - y[3]) * inverse, (y[2] - y[0]) * inverse
        x31, x02 = (x[3] - x[1]) * inverse, (x[0] - x[2]) * inverse
        bx = [y13, y20, -y13, -y20]
        by = [x31, x02, -x31, -x02]
        u02, u13, v02, v13 = u[0] - u[2], u[1] - u[3], v[0] - v[2], v[1] - v[3]
        rate_xx = y13 * u02 + y20 * u13
        rate_yy = x31 * v02 + x02 * v13
        rate_xy = x31 * u02 + x02 * u13 + y13 * v02 + y20 * v13
        s0 = stress_ref[0, here, :] + TIME_STEP * (stiff * (rate_xx + POISSON * rate_yy))
        s1 = stress_ref[1, here, :] + TIME_STEP * (stiff * (POISSON * rate_xx + rate_yy))
        s2 = stress_ref[2, here, :] + TIME_STEP * (YOUNG / (2.0 * (1.0 + POISSON)) * rate_xy)
        new_ref[0, here, :] = s0
        new_ref[1, here, :] = s1
        new_ref[2, here, :] = s2
        half_area = 0.5 * twice_area
        hour_x = x[0] - x[1] + x[2] - x[3]
        hour_y = y[0] - y[1] + y[2] - y[3]
        shape = [HOUR_SIGNS[i] - hour_x * bx[i] - hour_y * by[i] for i in range(4)]
        rate = tuple(
            HOURGLASS * sum(shape[i] * speed[i][c] for i in range(4)) for c in range(3)
        )
        for i in range(4):
            force_x = half_area * (bx[i] * s0 + by[i] * s2)
            force_y = half_area * (by[i] * s1 + bx[i] * s2)
            start = (group * 32 + i) * ROWS
            for c in range(3):
                internal = force_x * axis_one[c] + force_y * axis_two[c] + shape[i] * rate[c]
                high, low = split_two(-internal)
                push_ref[pl.ds(start + c, 8, stride=4 * ROWS), :] = high
                push_ref[pl.ds(start + 3 + c, 8, stride=4 * ROWS), :] = low
            for c in range(6, ROWS):
                push_ref[pl.ds(start + c, 8, stride=4 * ROWS), :] = jnp.zeros((8, SEG), F32)


def product_tiles(value, turn):
    parts = split_three(value)
    order = (0, 0, 1, 0, 1, 2) if turn else (0, 1, 0, 2, 1, 0)
    return [parts[index] for index in order]


def row_mix(three, extras):
    width = three.shape[1]
    rows = [three] + extras
    pad = -sum(part.shape[0] for part in rows) % ROWS
    if pad:
        rows.append(jnp.zeros((pad, width), F32))
    return jnp.concatenate(rows, axis=0)


def node_features(place):
    ones = jnp.ones((3, place.shape[1]), F32)
    square = jnp.concatenate(
        split_three(place[0:1] ** 2 + place[1:2] ** 2 + place[2:3] ** 2), axis=0
    )
    tiles = product_tiles(place, True)
    return row_mix(tiles[0], tiles[1:] + [ones]), row_mix(tiles[0], tiles[1:] + [ones, square])


def segment_features(centre, normal):
    ones = jnp.ones((3, centre.shape[1]), F32)
    lean = centre[0:1] * normal[0:1] + centre[1:2] * normal[1:2] + centre[2:3] * normal[2:3]
    lean = jnp.concatenate(split_three(-lean), axis=0)
    square = centre[0:1] ** 2 + centre[1:2] ** 2 + centre[2:3] ** 2
    square = jnp.concatenate(split_three(square), axis=0)
    tiles = product_tiles(normal, False)
    gap = row_mix(tiles[0], tiles[1:] + [lean])
    tiles = product_tiles(-2.0 * centre, False)
    return gap, row_mix(tiles[0], tiles[1:] + [square, ones])


FEATURES = 6 * ROWS
SCALE = math.sqrt(math.log2(math.e) / REACH)


def feature_kernel(step, own_ref, mask_ref, node_ref):
    cands = mask_ref.shape[1]

    def features(index, carry):
        start = pl.multiple_of(index * SEG, SEG)
        gap, far = node_features(own_ref[0:3, pl.ds(start, SEG)] * SCALE)
        mask = mask_ref[step, :, pl.ds(start, SEG)].astype(F32)
        for k in range(cands):
            live = mask[k : k + 1]
            rows = jnp.concatenate([gap * live, far], axis=0)
            rows = jnp.concatenate([rows, jnp.zeros((SEG - FEATURES, SEG), F32)], axis=0)
            node_ref[k, pl.ds(start, SEG), :] = rows.T.astype(BF16)
        return carry

    lax.fori_loop(0, own_ref.shape[1] // SEG, features, 0, unroll=2)


def contact_kernel(
    step, list_any, node_ref, slots_ref, force_ref, react_ref, seg_ref, push_ref, list_ref, sem
):
    fetch = pltpu.make_async_copy(list_any, list_ref, sem)
    fetch.start()
    buckets = node_ref.shape[1] // SEG
    cands = node_ref.shape[0]
    slots = react_ref.shape[0]
    react_ref[...] = jnp.zeros_like(react_ref)

    peers, groups = slots_ref.shape[:2]
    per_peer = slots // peers
    for index in range(slots):
        if index % per_peer == 0:
            rows = [slots_ref[index // per_peer, group] for group in range(groups)]
            rows = jnp.concatenate(rows, axis=0)
        tile = rows[index % per_peer * SENT : (index % per_peer + 1) * SENT]
        gap, far = segment_features(tile[0:3] * SCALE, tile[3:6])
        blank = jnp.zeros((FEATURES // 2, SEG), F32)
        left = jnp.concatenate([gap, blank], axis=0)
        right = jnp.concatenate([blank, far], axis=0)
        seg_ref[index] = jnp.concatenate([left, right], axis=1).astype(BF16)
        push = split_rows(tile[3:6])
        push = jnp.concatenate([push, push], axis=1)
        push_ref[index] = jnp.concatenate([push, jnp.zeros_like(push)], axis=0).astype(BF16)
    fetch.wait()

    def bucket(index, carry):
        start = pl.multiple_of(index * SEG, SEG)
        chosen = [list_ref[step, k, index] for k in range(cands)]
        pairs = [
            jnp.dot(
                node_ref[k, pl.ds(start, SEG), :][:, :FEATURES],
                seg_ref[chosen[k]],
                preferred_element_type=F32,
            )
            for k in range(cands)
        ]
        parts = []
        for k in range(cands):
            gap, far = pairs[k][:, :SEG], pairs[k][:, SEG:]
            weight = jnp.minimum(gap, 0.0) * jnp.exp2(gap * gap - far)
            react_ref[pl.ds(chosen[k], 1), :] += jnp.sum(weight, axis=0, keepdims=True)
            high = weight.astype(BF16)
            low = (weight - high.astype(F32)).astype(BF16)
            parts.append(jnp.concatenate([high, low], axis=1))
        total = dot_rows(
            jnp.concatenate([push_ref[slot] for slot in chosen], axis=1),
            jnp.concatenate(parts, axis=1),
        )
        force = (total[0:3] + total[3:6]) * (-PENALTY / SCALE)
        force_ref[:, pl.ds(start, SEG)] = row_mix(force, [])
        return carry

    lax.fori_loop(0, buckets, bucket, 0, unroll=16)
    react_ref[...] = react_ref[...] * (-PENALTY / SCALE)


def internal_kernel(rows_ref, conn_ref, acc_ref):
    scatter_tiles(rows_ref, conn_ref, acc_ref)


def pick_kernel(picks_ref, conn_ref, tiles_ref):
    for step in range(tiles_ref.shape[0]):

        def copy(slot, carry):
            tiles_ref[step, slot] = corner_ids(conn_ref, picks_ref[step, slot])
            return carry

        lax.fori_loop(0, tiles_ref.shape[1], copy, 0, unroll=8)


def collect_kernel(step, picks_ref, back_ref, seg_ref):
    seg_ref[...] = jnp.zeros_like(seg_ref)

    def collect(slot, carry):
        seg_ref[pl.ds(picks_ref[step, slot], 1), :] += back_ref[pl.ds(slot, 1), :]
        return carry

    lax.fori_loop(0, back_ref.shape[0], collect, 0)


def react_tiles(step, first, last, low, unroll, blocks_ref, back_ref, tiles_ref):
    def tile(index, total):
        react = back_ref[pl.ds(index, 1), :]
        normal = blocks_ref[pl.ds(pl.multiple_of(index * ROWS, ROWS), ROWS), :][3:6]
        rows = split_rows(-0.25 * react * normal)
        values = jnp.concatenate([rows, rows], axis=1)
        corners = tiles_ref[step, index]
        for half in range(2):
            ids = pair_row(corners, half)
            spread = spread_rows(values, ids, first, last, low)
            total = total + dot_rows(spread, one_hot_low(ids & (low - 1), low))
        return total

    start = jnp.zeros(((last - first) * ROWS, low), F32)
    return lax.fori_loop(0, back_ref.shape[0], tile, start, unroll=unroll)


def unstack(total):
    count = total.shape[0] // ROWS
    full = jnp.concatenate(
        [total[part * ROWS : (part + 1) * ROWS] for part in range(count)], axis=1
    )
    return row_mix(full[0:3] + full[3:6], [])


def react_ghost_kernel(step, blocks_ref, back_ref, tiles_ref, acc_ref, mesh_ref, sub_ref):
    count = acc_ref.shape[0] // ROWS
    ghosts = mesh_ref.shape[1] + sub_ref.shape[1]
    first, last = count * LOW // SEG - ghosts // SEG, count * LOW // SEG
    total = react_tiles(step, first, last, SEG, 16, blocks_ref, back_ref, tiles_ref)
    full = unstack(total) + unstack(acc_ref[(count - ghosts // LOW) * ROWS :, :])
    mesh_ref[...] = full[:4, : mesh_ref.shape[1]]
    sub_ref[...] = full[:4, mesh_ref.shape[1] :]


def react_own_kernel(step, blocks_ref, back_ref, tiles_ref, acc_ref, own_ref):
    nodes = own_ref.shape[1]
    total = react_tiles(step, 0, nodes // SEG, SEG, 16, blocks_ref, back_ref, tiles_ref)
    own_ref[...] = unstack(total) + unstack(acc_ref[: nodes // LOW * ROWS, :])


def spread_rows(values, ids, first, last, low=LOW):
    width = values.shape[1]
    twice = jnp.concatenate([values, values], axis=0).astype(BF16)
    high_ids = jnp.broadcast_to((ids >> (low.bit_length() - 1)).astype(F32), (2 * ROWS, width))
    second = lax.broadcasted_iota(jnp.int32, (2 * ROWS, width), 0) >= ROWS
    offset = (high_ids - jnp.where(second, 1.0, 0.0)).astype(BF16)
    zero = jnp.zeros((), BF16)
    parts = [
        jnp.where(offset == jnp.asarray(part, BF16), twice, zero) for part in range(first, last, 2)
    ]
    return jnp.concatenate(parts, axis=0)


def dot_rows(left, right):
    return lax.dot_general(left, right, (((1,), (1,)), ((), ())), preferred_element_type=F32)


def scatter_tiles(rows_ref, conn_ref, acc_ref):
    count = acc_ref.shape[0] // ROWS
    acc_ref[...] = jnp.zeros_like(acc_ref)

    def tile(block, carry):
        corners = corner_ids(conn_ref, block)
        for half in range(2):
            ids = pair_row(corners, half)
            start = pl.multiple_of((block * 2 + half) * 2 * ROWS, 2 * ROWS)
            parts = [rows_ref[pl.ds(start + i * ROWS, ROWS), :] for i in range(2)]
            spread = spread_rows(jnp.concatenate(parts, axis=1), ids, 0, count)
            acc_ref[...] += dot_rows(spread, one_hot_low(ids & (LOW - 1)))
        return carry

    lax.fori_loop(0, conn_ref.shape[1] // SEG, tile, 0, unroll=UNROLL // 2)


def add_back(back, ids_ref, count):
    rows = split_rows(back[0:3])
    total = jnp.zeros((count * ROWS, SEG), F32)
    for index in range(back.shape[1] // LOW):
        here = slice(index * LOW, (index + 1) * LOW)
        ids = ids_ref[:, here]
        spread = spread_rows(rows[:, here], ids, 0, count, SEG)
        total = total + dot_rows(spread, one_hot_low(ids & (SEG - 1), SEG))
    return total


def pack_ghosts(table, ids_ref, out_ref):
    count = table.shape[0] // (3 * ROWS)
    size = count * ROWS
    for index in range(out_ref.shape[1] // LOW):
        here = slice(index * LOW, (index + 1) * LOW)
        ids = ids_ref[:, here]
        product = jnp.dot(table, one_hot_low(ids & (LOW - 1)), preferred_element_type=F32)
        product = product[:size] + product[size : 2 * size] + product[2 * size :]
        out_ref[:, here] = pick_high(product, ids >> 8, count)


def pack_both(own, mesh_ids_ref, sub_ids_ref, to_mesh_ref, to_sub_ref):
    parts = [stack_columns(part) for part in split_three(own)]
    table = jnp.concatenate(parts, axis=0).astype(BF16)
    pack_ghosts(table, mesh_ids_ref, to_mesh_ref)
    pack_ghosts(table, sub_ids_ref, to_sub_ref)


def pack_kernel(
    coords_any, veloc_any, mesh_any, sub_any, own_ref, to_mesh_ref, to_sub_ref, coords_ref,
    veloc_ref, mesh_ids_ref, sub_ids_ref, sems,
):
    sources = (coords_any, veloc_any, mesh_any, sub_any)
    targets = (coords_ref, veloc_ref, mesh_ids_ref, sub_ids_ref)
    copies = [
        pltpu.make_async_copy(source, target, sems.at[index])
        for index, (source, target) in enumerate(zip(sources, targets))
    ]
    for copy in copies:
        copy.start()
    for copy in copies:
        copy.wait()
    pad = jnp.zeros((ROWS - 6, coords_ref.shape[1]), F32)
    own = jnp.concatenate([coords_ref[...], veloc_ref[...], pad], axis=0)
    own_ref[...] = own
    pack_both(own, mesh_ids_ref, sub_ids_ref, to_mesh_ref, to_sub_ref)


def new_state(
    own_ref, force_ref, slave_ref, back_mesh_ref, back_sub_ref, mass_ref, mesh_ids_ref,
    sub_ids_ref,
):
    count = own_ref.shape[1] // SEG
    extra = add_back(back_mesh_ref[...], mesh_ids_ref, count) + add_back(
        back_sub_ref[...], sub_ids_ref, count
    )
    full = unstack(extra)
    force = force_ref[0:3, :] + slave_ref[0:3, :] + full[0:3]
    return own_ref[3:6, :] + TIME_STEP * force / mass_ref[...]


def update_kernel(*refs):
    own_ref, mesh_ids_ref, sub_ids_ref = refs[0], refs[6], refs[7]
    new_ref, to_mesh_ref, to_sub_ref = refs[8:]
    speed = new_state(*refs[:8])
    place = own_ref[0:3, :] + TIME_STEP * speed
    own = jnp.concatenate([place, speed, jnp.zeros((ROWS - 6, place.shape[1]), F32)], axis=0)
    new_ref[...] = own
    pack_both(own, mesh_ids_ref, sub_ids_ref, to_mesh_ref, to_sub_ref)


def last_kernel(*refs):
    refs[8][...] = new_state(*refs[:8])


VM = pl.BlockSpec(memory_space=pltpu.VMEM)
SM = pl.BlockSpec(memory_space=pltpu.SMEM)
ANY = pl.BlockSpec(memory_space=pl.ANY)
HBM = pl.BlockSpec(memory_space=pltpu.HBM)


def call(kernel, outs, ins, scratch=(), flops=0):
    shapes = tuple(
        jax.ShapeDtypeStruct(shape, F32) if isinstance(shape, tuple) else shape for shape in outs
    )
    return pl.pallas_call(
        kernel,
        out_shape=shapes,
        in_specs=list(ins),
        out_specs=tuple(VM for _ in outs),
        scratch_shapes=[
            pltpu.VMEM(shape, F32) if isinstance(shape, tuple) else shape for shape in scratch
        ],
        compiler_params=pltpu.CompilerParams(vmem_limit_bytes=8 << 20),
        cost_estimate=pl.CostEstimate(flops=flops, bytes_accessed=1 << 20, transcendentals=0),
    )


def per_device(
    coords,
    veloc,
    node_mass,
    stress,
    connect,
    send_mesh,
    send_sub,
    send_pick,
    bucket_list,
    pair_mask,
):
    nodes = coords.shape[1]
    elems = stress.shape[1]
    ghost_mesh = send_mesh.shape[0]
    ghost_sub = send_sub.shape[0]
    width = nodes + ghost_mesh + ghost_sub
    peers = lax.axis_size("mesh")
    slots = send_pick.shape[1]
    per_peer = slots // peers
    blocks = elems // SEG
    mesh_ids = send_mesh.reshape(1, ghost_mesh)
    sub_ids = send_sub.reshape(1, ghost_sub)
    mass = node_mass.reshape(1, nodes)
    stress_now = stress.reshape(3, blocks, SEG)
    conn = connect

    chunks = nodes // SEG
    ghost_chunks = (ghost_mesh + ghost_sub) // SEG
    cands = bucket_list.shape[1]

    pack = call(
        pack_kernel,
        [
            (ROWS, nodes),
            (ROWS, ghost_mesh),
            (ROWS, ghost_sub),
        ],
        [HBM] * 4,
        [
            (3, nodes),
            (3, nodes),
            pltpu.VMEM((1, ghost_mesh), jnp.int32),
            pltpu.VMEM((1, ghost_sub), jnp.int32),
            pltpu.SemaphoreType.DMA((4,)),
        ],
    )
    own_rows_of = call(
        own_rows_kernel, [(2 * blocks * ROWS, SEG)], [VM] * 2, [(chunks, ROWS, SEG)], flops=1 << 31
    )
    by_slot = slots <= blocks
    geom = lambda step: call(
        functools.partial(
            geometry_slots_kernel if by_slot else geometry_blocks_kernel, step, nodes
        ),
        [
            (12, blocks, SEG),
            (slots * ROWS if by_slot else blocks * ROWS, SEG),
            (peers, pl.cdiv(per_peer * SENT, 4), 4, SEG),
        ],
        [ANY] + [VM] * 4,
        ([(blocks * ROWS, SEG)] if by_slot else [])
        + [
            (2 * blocks * ROWS, SEG),
            (ghost_chunks, ROWS, SEG),
            pltpu.SMEM(send_pick.shape, jnp.int32),
            pltpu.SemaphoreType.DMA,
        ],
        flops=1 << 30,
    )
    forces = call(
        force_kernel,
        [(4 * blocks * ROWS, SEG), (3, blocks, SEG)],
        [VM] * 6,
        [(4 * blocks * ROWS, SEG)],
        flops=1 << 31,
    )
    features = lambda step: call(
        functools.partial(feature_kernel, step),
        [jax.ShapeDtypeStruct((cands, nodes, SEG), BF16)],
        [VM] * 2,
        flops=1 << 30,
    )
    contact = lambda step: call(
        functools.partial(contact_kernel, step),
        [(ROWS, nodes), (slots, SEG)],
        [ANY] + [VM] * 2,
        [
            pltpu.VMEM((slots, FEATURES, 2 * SEG), BF16),
            pltpu.VMEM((slots, 2 * ROWS, 2 * SEG), BF16),
            pltpu.SMEM(bucket_list.shape, jnp.int32),
            pltpu.SemaphoreType.DMA,
        ],
        flops=1 << 31,
    )
    internal_of = call(internal_kernel, [(width // LOW * ROWS, LOW)], [VM] * 2, flops=1 << 31)
    react_ghost = lambda step: call(
        functools.partial(react_ghost_kernel, step),
        [(4, ghost_mesh), (4, ghost_sub)],
        [VM] * 4,
        flops=1 << 29,
    )
    react_own = lambda step: call(
        functools.partial(react_own_kernel, step), [(ROWS, nodes)], [VM] * 4, flops=1 << 30
    )
    update = call(update_kernel, [(ROWS, nodes), (ROWS, ghost_mesh), (ROWS, ghost_sub)], [VM] * 8)
    finish = call(last_kernel, [(3, nodes)], [VM] * 8)

    pick_tiles = call(
        pick_kernel,
        [jax.ShapeDtypeStruct((STEPS, slots, 4, SEG), jnp.int32)],
        [SM, VM],
        flops=1 << 20,
    )
    collect = lambda step: call(functools.partial(collect_kernel, step), [(blocks, SEG)], [SM, VM])

    own, to_mesh, to_sub = pack(
        *[
            pltpu.with_memory_space_constraint(source, pltpu.HBM)
            for source in (coords, veloc, mesh_ids, sub_ids)
        ]
    )
    if by_slot:
        (tiles,) = pick_tiles(send_pick, conn)
    else:
        tiles = conn.reshape(4, blocks, SEG).transpose(1, 0, 2)[None]
    for step in range(STEPS):
        from_mesh = shifted(to_mesh, "mesh", 1)
        from_sub = shifted(to_sub, "sub", 1)
        (own_rows,) = own_rows_of(own, conn)
        (node,) = features(step)(own, pair_mask)
        corner, kept, outgoing = geom(step)(
            send_pick, from_mesh, from_sub, conn, own_rows
        )
        incoming = lax.all_to_all(
            outgoing, "mesh", split_axis=0, concat_axis=0, tiled=True
        )
        pushes, stress_now = forces(own, from_mesh, from_sub, conn, corner, stress_now)
        slave, react = contact(step)(bucket_list, node, incoming)
        returned = lax.all_to_all(
            react.reshape(peers, per_peer, SEG),
            "mesh", split_axis=0, concat_axis=0, tiled=True,
        ).reshape(slots, SEG)
        (acc,) = internal_of(pushes, conn)
        at = step if by_slot else 0
        if by_slot:
            rows = (kept, returned, tiles, acc)
        else:
            rows = (kept, collect(step)(send_pick, returned)[0], tiles, acc)
        back_mesh, back_sub = react_ghost(at)(*rows)
        (force,) = react_own(at)(*rows)
        back_mesh = shifted(back_mesh, "mesh", -1)
        back_sub = shifted(back_sub, "sub", -1)
        args = (own, force, slave, back_mesh, back_sub, mass, mesh_ids, sub_ids)
        if step < STEPS - 1:
            own, to_mesh, to_sub = update(*args)
        else:
            (own,) = finish(*args)
    return own, stress_now.reshape(3, elems)


def solution(mesh):
    return jax.shard_map(
        per_device,
        mesh=mesh,
        in_specs=(
            P(None, ("mesh", "sub")),
            P(None, ("mesh", "sub")),
            P(("mesh", "sub")),
            P(None, ("mesh", "sub")),
            P(None, ("mesh", "sub")),
            P(("mesh", "sub")),
            P(("mesh", "sub")),
            P(None, ("mesh", "sub")),
            P(None, None, ("mesh", "sub")),
            P(None, None, ("mesh", "sub")),
        ),
        out_specs=(P(None, ("mesh", "sub")), P(None, ("mesh", "sub"))),
        check_vma=False,
    )
```
